32 devices in a mesh: dp: 8 (over z, y), tensor: 4 (over x, core).
Axes of the slice: x: 2, y: 2, z: 4, core: 2. Of those that a mesh axis runs over, the one named last changes fastest.
Arguments:
- inputs: bfloat16 [16, 1024, 768], P('dp', 'tensor'), may hold values from -6 to 6
- segment_ids: int32 [16, 1024], P('dp'), may hold values from 0 to 11, never falling along the last dimension, each value on 1 to 512 neighbouring positions
- cotangent: bfloat16 [16, 1024, 768], P('dp', 'tensor'), may hold values from -6 to 6
- w_query: bfloat16 [768, 768], P(None, 'tensor'), may hold values from -0.21875 to 0.21875
- w_key: bfloat16 [768, 768], P(None, 'tensor'), may hold values from -0.21875 to 0.21875
- w_value: bfloat16 [768, 768], P(None, 'tensor'), may hold values from -0.21875 to 0.21875
- b_query: float32 [768], P('tensor'), may hold values from -3 to 3
- b_value: float32 [768], P('tensor'), may hold values from -3 to 3
- w_out: bfloat16 [768, 768], P('tensor'), may hold values from -1.25 to 1.25
- b_out: float32 [768], replicated, may hold values from -2 to 2
- gain_one: float32 [768], replicated, may hold values from 0.5 to 1.5
- shift_one: float32 [768], replicated, may hold values from -2 to 2
- w_up: bfloat16 [768, 3072], P(None, 'tensor'), may hold values from -0.21875 to 0.21875
- b_up: float32 [3072], P('tensor'), may hold values from -3 to 3
- w_down: bfloat16 [3072, 768], P('tensor'), may hold values from -0.109375 to 0.109375
- b_down: float32 [768], replicated, may hold values from -2 to 2
- gain_two: float32 [768], replicated, may hold values from 0.5 to 1.5
- shift_two: float32 [768], replicated, may hold values from -2 to 2
Outputs:
- output: bfloat16 [16, 1024, 768], P('dp', 'tensor')
- grad_input: float32 [16, 1024, 768], P('dp', 'tensor')
- grad_w_query: float32 [768, 768], P(None, 'tensor')
- grad_w_key: float32 [768, 768], P(None, 'tensor')
- grad_w_value: float32 [768, 768], P(None, 'tensor')
- grad_b_query: float32 [768], P('tensor')
- grad_b_value: float32 [768], P('tensor')
- grad_w_out: float32 [768, 768], P('tensor')
- grad_b_out: float32 [768], replicated
- grad_gain_one: float32 [768], replicated
- grad_shift_one: float32 [768], replicated
- grad_w_up: float32 [768, 3072], P(None, 'tensor')
- grad_b_up: float32 [3072], P('tensor')
- grad_w_down: float32 [3072, 768], P('tensor')
- grad_b_down: float32 [768], replicated
- grad_gain_two: float32 [768], replicated
- grad_shift_two: float32 [768], replicated
The draws below stay inside these ranges and needn't reach their ends.
Inputs may be any that keep to these rules, and one draw needn't show every extreme that they name: `segment_ids`: along each sequence the ids never fall; each of the 12 documents of a sequence holds 1 to 512 consecutive tokens, and some document has exactly 512 of them.
All inputs are finite; a program needn't handle non-finite values.
Results may differ from the reference program's by a relative error of at most 0.018.
Values may be sent and summed in bfloat16 or wider, within the bound.
No kernel may reach another device: no remote copies, remote signals or barrier semaphores. Data moves between devices by JAX's collectives and lax.ppermute only.
A program may use at most 128 MiB of HBM per device.

```python
import math
import jax
import jax.numpy as jnp
import numpy as np
from jax import lax

D = 768
HEADS = 12
HEAD_DIM = 64
FF = 3072
SEQ = 1024
SEQS = 16


def levels(own_key, extent, shards, low, largest):
    level, own = 1.0, jax.random.fold_in(own_key, 6)
    for axis_at, shards_of in shards:
        heights = jnp.exp(jax.random.uniform(jax.random.fold_in(own, axis_at), (shards_of,), jnp.float32, low / len(shards), largest / len(shards)))
        level = level * jnp.repeat(heights, extent[axis_at] // shards_of).reshape([-1 if axis == axis_at else 1 for axis in range(len(extent))])
    return level


def split_up(number_of, total, reach, lean):
    weights = [(1 << 20) // math.isqrt(standing ** lean) + 1 for standing in range(2, number_of + 1)]
    surplus, given = total - reach - (number_of - 1), [1] * (number_of - 1)
    while surplus > 0:
        free = [i for i in range(number_of - 1) if given[i] < reach]
        whole, remaining = sum([weights[i] for i in free]), surplus
        for i in free:
            extra = min(reach - given[i], max(1, remaining * weights[i] // whole), surplus)
            given[i] = given[i] + extra
            surplus = surplus - extra
    return np.array([reach] + given)


def ragged(stream_key, count, total, limit, slope):
    if count == 2:
        one = jax.random.randint(stream_key, (), max(1, total - limit), min(limit, total - 1) + 1)
        return jnp.stack([one, total - one])
    tallies = jnp.asarray(split_up(count, total, limit, slope), jnp.int32)
    twos = (count - 1) // 2
    giver, taker = tallies[1:1 + 2 * twos:2], tallies[2:2 + 2 * twos:2]
    slack = jnp.minimum(giver - 1, limit - taker)
    moved = jax.random.randint(jax.random.fold_in(stream_key, 1), (twos,), 0, 1 << 20) % (slack + 1)
    tallies = tallies.at[1:1 + 2 * twos:2].set(giver - moved).at[2:2 + 2 * twos:2].set(taker + moved)
    return tallies[jax.random.permutation(jax.random.fold_in(stream_key, 2), count)]


def normal_values(key, extent, spread, reach, shards=(), dtype=jnp.bfloat16):
    level = levels(key, extent, shards, -0.22, 0.18) if shards else 1.0
    result = jax.random.normal(key, extent, jnp.float32) * spread * level
    return jnp.minimum(jnp.maximum(result, -reach), reach).astype(dtype)


def setup_inputs(seed: int = 0) -> dict:
    seeds = jax.random.split(jax.random.key(seed), 19)
    return {
        "inputs": normal_values(seeds[0], (SEQS, SEQ, D), 1.0, 6.0, ((0, 8), (1, 4))),
        "segment_ids": jax.vmap(lambda own: jnp.searchsorted(jnp.cumsum(ragged(own, 12, SEQ, SEQ // 2, 2)), jnp.arange(SEQ), side="right"))(jax.random.split(seeds[1], SEQS)).reshape((SEQS, SEQ)).astype(jnp.int32),
        "cotangent": normal_values(seeds[2], (SEQS, SEQ, D), 1.0, 6.0, ((0, 8), (1, 4))),
        "w_query": normal_values(seeds[3], (D, D), D ** -0.5, 0.21875, ((1, 4),)),
        "w_key": normal_values(seeds[4], (D, D), D ** -0.5, 0.21875, ((1, 4),)),
        "w_value": normal_values(seeds[5], (D, D), D ** -0.5, 0.21875, ((1, 4),)),
        "b_query": normal_values(seeds[6], (D,), 0.5, 3.0, ((0, 4),), jnp.float32),
        "b_value": normal_values(seeds[7], (D,), 0.5, 3.0, ((0, 4),), jnp.float32),
        "w_out": normal_values(seeds[8], (D, D), (D // 32) ** -0.5, 1.25, ((0, 4),)),
        "b_out": normal_values(seeds[9], (D,), 0.3, 2.0, (), jnp.float32),
        "gain_one": jnp.clip(1.0 + 0.1 * jax.random.normal(seeds[10], (D,), jnp.float32), 0.5, 1.5),
        "shift_one": normal_values(seeds[11], (D,), 0.3, 2.0, (), jnp.float32),
        "w_up": normal_values(seeds[12], (D, FF), D ** -0.5, 0.21875, ((1, 4),)),
        "b_up": normal_values(seeds[13], (FF,), 0.5, 3.0, ((0, 4),), jnp.float32),
        "w_down": normal_values(seeds[14], (FF, D), FF ** -0.5, 0.109375, ((0, 4),)),
        "b_down": normal_values(seeds[15], (D,), 0.3, 2.0, (), jnp.float32),
        "gain_two": jnp.clip(1.0 + 0.1 * jax.random.normal(seeds[16], (D,), jnp.float32), 0.5, 1.5),
        "shift_two": normal_values(seeds[17], (D,), 0.3, 2.0, (), jnp.float32),
    }


@jax.custom_vjp
def low(v):
    return lax.optimization_barrier(v.astype(jnp.bfloat16)).astype(jnp.float32)

@jax.custom_vjp
def low_back(v):
    return v

def low_keep(v):
    return (low(v), None)

def low_pass(kept, grad):
    return (grad,)

def back_keep(v):
    return (v, None)

def back_low(kept, grad):
    return (low(grad),)
low.defvjp(low_keep, low_pass)
low_back.defvjp(back_keep, back_low)
LAYER_EPSILON = 1e-05
HIGHEST_PRECISION = lax.Precision.HIGHEST

def rounded_both(value):
    return low_back(low(value))

def layer_norm(rows, gain, shift):
    average = lax.optimization_barrier(jnp.mean(rows, -1, keepdims=True))
    centred = rows - average
    variance = lax.optimization_barrier(jnp.mean(centred * centred, -1, keepdims=True))
    return centred * lax.rsqrt(variance + LAYER_EPSILON) * gain + shift

def sequence_forward(inputs, segment_row, params):
    w_query, w_key, w_value, b_query, b_value, w_out, b_out, gain_one, shift_one, w_up, b_up, w_down, b_down, gain_two, shift_two = params
    length = inputs.shape[0]
    score_scale = 1.0 / math.sqrt(HEAD_DIM)

    def project(weight):
        return jnp.dot(inputs, weight, precision=HIGHEST_PRECISION)
    query = rounded_both(project(w_query) + b_query).reshape(length, HEADS, HEAD_DIM)
    keys = rounded_both(project(w_key)).reshape(length, HEADS, HEAD_DIM)
    values = rounded_both(project(w_value) + b_value).reshape(length, HEADS, HEAD_DIM)
    scores = low_back(jnp.einsum('qhd,khd->hqk', query, keys, precision=HIGHEST_PRECISION) * score_scale)
    same_doc = segment_row[:, None] == segment_row[None, :]
    scores = jnp.where(same_doc[None], scores, -1e+30)
    attention = jax.nn.softmax(scores, axis=-1)
    context = jnp.einsum('hqk,khd->qhd', low(attention), values, precision=HIGHEST_PRECISION)
    context = rounded_both(context.reshape(length, HEADS * HEAD_DIM))
    attended = low_back(jnp.dot(context, w_out, precision=HIGHEST_PRECISION) + b_out)
    hidden_one = layer_norm(inputs + attended, gain_one, shift_one)
    before_gelu = low_back(jnp.dot(low(hidden_one), w_up, precision=HIGHEST_PRECISION) + b_up)
    activation = low(jax.nn.gelu(before_gelu, approximate=True))
    branch = low_back(jnp.dot(activation, w_down, precision=HIGHEST_PRECISION) + b_down)
    return layer_norm(hidden_one + branch, gain_two, shift_two)

def reference(inputs, segment_ids, cotangent, w_query, w_key, w_value, b_query, b_value, w_out, b_out, gain_one, shift_one, w_up, b_up, w_down, b_down, gain_two, shift_two):
    params = tuple((weight.astype(jnp.float32) for weight in (w_query, w_key, w_value, b_query, b_value, w_out, b_out, gain_one, shift_one, w_up, b_up, w_down, b_down, gain_two, shift_two)))

    def one_sequence(running, sequence_item):
        input_row, segment_row, cotangent_row = sequence_item

        def forward(values_in, params_in):
            return sequence_forward(values_in, segment_row, params_in)
        output, pullback = jax.vjp(forward, input_row.astype(jnp.float32), params)
        grad_input, grad_params = pullback(cotangent_row.astype(jnp.float32))
        running = jax.tree.map(lambda accumulated, addition: accumulated + addition, running, grad_params)
        return (running, (output.astype(jnp.bfloat16), grad_input))
    zero_grads = jax.tree.map(jnp.zeros_like, params)
    totals, (outputs, grad_inputs) = lax.scan(one_sequence, zero_grads, (inputs, segment_ids, cotangent))
    return (outputs, grad_inputs, totals[0], totals[1], totals[2], totals[3], totals[4], totals[5], totals[6], totals[7], totals[8], totals[9], totals[10], totals[11], totals[12], totals[13], totals[14])
```

```python
import math

import jax
import jax.numpy as jnp
from jax import lax
from jax.sharding import PartitionSpec as P

HEAD_DIM = 64
LAYER_EPSILON = 1e-05
BF = jnp.bfloat16
F32 = jnp.float32


def dot(left, right, contract):
    return lax.dot_general(left, right, (contract, ((), ())), preferred_element_type=F32)


def mm(left, right):
    return dot(left, right, ((1,), (0,)))


def mm_t(left, right):
    return dot(left, right, ((1,), (1,)))


def t_mm(left, right):
    return dot(left, right, ((0,), (0,)))


def normalize(rows):
    centred = rows - jnp.mean(rows, -1, keepdims=True)
    inverse = lax.rsqrt(jnp.mean(centred * centred, -1, keepdims=True) + LAYER_EPSILON)
    return centred * inverse, inverse


def norm_backward(grad, gain, normal, inverse):
    scaled = grad * gain
    mean = jnp.mean(scaled, -1, keepdims=True)
    mean_z = jnp.mean(scaled * normal, -1, keepdims=True)
    return inverse * (scaled - mean - normal * mean_z), jnp.sum(grad * normal, 0), jnp.sum(grad, 0)


def gelu_pair(u):
    root = math.sqrt(2 / math.pi)
    t = jnp.tanh(root * (u + 0.044715 * u * u * u))
    value = 0.5 * u * (1 + t)
    slope = 0.5 * (1 + t) + 0.5 * u * (1 - t * t) * root * (1 + 3 * 0.044715 * u * u)
    return value, slope


def attention_forward(query, keys, values, seg_q, seg_k):
    scores = jnp.einsum("qhd,khd->hqk", query, keys, preferred_element_type=F32) / math.sqrt(HEAD_DIM)
    masked = jnp.where((seg_q[:, None] == seg_k[None, :])[None], scores, -1e30)
    top = jnp.max(masked, -1, keepdims=True)
    exponent = jnp.exp(masked - top)
    total = jnp.sum(exponent, -1, keepdims=True)
    weights = (exponent / total).astype(BF)
    context = jnp.einsum("hqk,khd->qhd", weights, values, preferred_element_type=F32)
    return context.astype(BF), top + jnp.log(total)


def attention_backward(query, keys, values, seg_q, seg_k, logsum, grad):
    scale = 1 / math.sqrt(HEAD_DIM)
    scores = jnp.einsum("qhd,khd->hqk", query, keys, preferred_element_type=F32) * scale
    masked = jnp.where((seg_q[:, None] == seg_k[None, :])[None], scores, -1e30)
    weights = jnp.exp(masked - logsum)
    grad_weights = jnp.einsum("qhd,khd->hqk", grad, values, preferred_element_type=F32)
    row = jnp.sum(weights * grad_weights, -1, keepdims=True)
    grad_scores = (weights * (grad_weights - row)).astype(BF)
    grad_query = jnp.einsum("hqk,khd->qhd", grad_scores, keys, preferred_element_type=F32) * scale
    grad_keys = jnp.einsum("hqk,qhd->khd", grad_scores, query, preferred_element_type=F32) * scale
    grad_values = jnp.einsum("hqk,qhd->khd", weights.astype(BF), grad, preferred_element_type=F32)
    return grad_query.astype(BF), grad_keys, grad_values


def shards(
    inputs,
    segment_ids,
    cotangent,
    w_query,
    w_key,
    w_value,
    b_query,
    b_value,
    w_out,
    b_out,
    gain_one,
    shift_one,
    w_up,
    b_up,
    w_down,
    b_down,
    gain_two,
    shift_two,
):
    ranks = lax.axis_size("tensor")
    rank = lax.axis_index("tensor")
    which = rank % 2
    rows = inputs.shape[1]
    half = 2 * rows
    width = w_query.shape[1]
    hidden_width = w_up.shape[1]
    model = inputs.shape[2]

    def inner(x):
        return lax.ppermute(x, "tensor", [(i, i ^ 1) for i in range(ranks)])

    def outer(x):
        return lax.ppermute(x, "tensor", [(i, i ^ 2) for i in range(ranks)])

    def to_sequence(x):
        kept = jnp.where(which == 0, x[0], x[1])
        got = inner(jnp.where(which == 0, x[1], x[0]))
        return jnp.where(which == 0, jnp.concatenate([kept, got]), jnp.concatenate([got, kept]))

    def from_sequence(x):
        low, high = x[:rows], x[rows:]
        kept = jnp.where(which == 0, low, high)
        got = inner(jnp.where(which == 0, high, low))
        return jnp.where(which == 0, jnp.stack([kept, got]), jnp.stack([got, kept]))

    own_in = to_sequence(inputs)
    other_in = outer(own_in)
    own_cot = to_sequence(cotangent).astype(F32)

    def both(x, axis):
        return jnp.concatenate([x, inner(x)], axis)

    wqkv = both(jnp.concatenate([w_query, w_key, w_value], 1)[None], 0)
    wqkv = wqkv.reshape(2, model, 3, width).transpose(1, 2, 0, 3).reshape(model, 3 * 2 * width)
    bias = both(jnp.stack([b_query, b_value])[None], 0).transpose(1, 0, 2).reshape(2, 2 * width)
    bias_qkv = jnp.concatenate([bias[0], jnp.zeros((2 * width,), F32), bias[1]])
    w_out2 = both(w_out, 0)
    w_up2 = both(w_up, 1)
    b_up2 = both(b_up, 0)
    w_down2 = both(w_down, 0)

    segments = jnp.where(which == 0, segment_ids[0], segment_ids[1])
    first = jnp.where(rank // 2 == 0, segments[:half], segments[half:])
    second = jnp.where(rank // 2 == 0, segments[half:], segments[:half])
    seg = jnp.concatenate([first, second])

    heads = 2 * width // HEAD_DIM

    def project(x):
        return (mm(x, wqkv) + bias_qkv).astype(BF)

    qkv = [project(own_in), project(other_in)]

    def split(x):
        return [x[:, i * 2 * width : (i + 1) * 2 * width].reshape(-1, heads, HEAD_DIM) for i in range(3)]

    pieces = [split(x) for x in qkv]
    keys = jnp.concatenate([pieces[0][1], pieces[1][1]])
    values = jnp.concatenate([pieces[0][2], pieces[1][2]])
    context_other, log_other = attention_forward(pieces[1][0], keys, values, second, seg)
    context_other = context_other.reshape(half, 2 * width)
    got = outer(mm(context_other, w_out2).astype(BF))
    context_own, log_own = attention_forward(pieces[0][0], keys, values, first, seg)
    context_own = context_own.reshape(half, 2 * width)
    attended = mm(context_own, w_out2) + got.astype(F32) + b_out
    normal_one, inverse_one = normalize(own_in.astype(F32) + attended)
    hidden_one = normal_one * gain_one + shift_one
    low_own = hidden_one.astype(BF)
    low_other = outer(low_own)

    def feed(low):
        value, slope = gelu_pair(mm(low, w_up2) + b_up2)
        return value.astype(BF), slope

    act_own, slope_own = feed(low_own)
    act_other, slope_other = feed(low_other)
    got = outer(mm(act_other, w_down2).astype(BF))
    branch = mm(act_own, w_down2) + got.astype(F32) + b_down
    normal_two, inverse_two = normalize(hidden_one + branch)
    output = (normal_two * gain_two + shift_two).astype(BF)

    grad_two, grad_gain_two, grad_shift_two = norm_backward(own_cot, gain_two, normal_two, inverse_two)
    gb_own = grad_two.astype(BF)
    grad_b_down = jnp.sum(gb_own.astype(F32), 0)
    gb_other = outer(gb_own)
    before_own = (mm_t(gb_own, w_down2) * slope_own).astype(BF)
    before_other = (mm_t(gb_other, w_down2) * slope_other).astype(BF)
    got = outer(mm_t(before_other, w_up2).astype(BF))
    grad_w_down = t_mm(act_own, gb_own) + t_mm(act_other, gb_other)
    grad_w_up = t_mm(low_own, before_own) + t_mm(low_other, before_other)
    grad_b_up = jnp.sum(before_own.astype(F32), 0) + jnp.sum(before_other.astype(F32), 0)
    grad_hidden = mm_t(before_own, w_up2) + got.astype(F32) + grad_two
    grad_one, grad_gain_one, grad_shift_one = norm_backward(grad_hidden, gain_one, normal_one, inverse_one)
    ga_own = grad_one.astype(BF)
    grad_b_out = jnp.sum(ga_own.astype(F32), 0)
    ga_other = outer(ga_own)

    def pair_sum(mine, theirs):
        return mine + inner(theirs.astype(BF)).astype(F32)

    grad_w_up = pair_sum(grad_w_up[:, :hidden_width], grad_w_up[:, hidden_width:])
    grad_w_down = pair_sum(grad_w_down[:hidden_width], grad_w_down[hidden_width:])
    feed_flat = jnp.concatenate([grad_w_up.astype(BF), grad_w_down.astype(BF)])
    feed_flat = lax.psum(feed_flat, "dp")

    gc_own = mm_t(ga_own, w_out2).astype(BF)
    gc_other = mm_t(ga_other, w_out2).astype(BF)
    grad_w_out = t_mm(context_own, ga_own) + t_mm(context_other, ga_other)
    shaped = (half, heads, HEAD_DIM)
    gq_own, gk_a, gv_a = attention_backward(
        pieces[0][0], keys, values, first, seg, log_own, gc_own.reshape(shaped)
    )
    gq_other, gk_b, gv_b = attention_backward(
        pieces[1][0], keys, values, second, seg, log_other, gc_other.reshape(shaped)
    )
    flat = (2 * half, 2 * width)
    gk = (gk_a + gk_b).astype(BF).reshape(flat)
    gv = (gv_a + gv_b).astype(BF).reshape(flat)
    gq_own = gq_own.reshape(half, 2 * width)
    gq_other = gq_other.reshape(half, 2 * width)
    gqkv_own = jnp.concatenate([gq_own, gk[:half], gv[:half]], 1)
    gqkv_other = jnp.concatenate([gq_other, gk[half:], gv[half:]], 1)
    got = outer(mm_t(gqkv_other, wqkv).astype(BF))
    grad_wqkv = t_mm(own_in, gqkv_own) + t_mm(other_in, gqkv_other)
    grad_bqkv = jnp.sum(gqkv_own.astype(F32), 0) + jnp.sum(gqkv_other.astype(F32), 0)
    grad_input = mm_t(gqkv_own, wqkv) + got.astype(F32) + grad_one

    by_part = grad_wqkv.reshape(model, 3, 2, width)
    grad_wqkv = pair_sum(
        by_part[:, :, 0].reshape(model, 3 * width), by_part[:, :, 1].reshape(model, 3 * width)
    )
    grad_w_out = pair_sum(grad_w_out[:width], grad_w_out[width:])
    attention_flat = jnp.concatenate([grad_wqkv.astype(BF).reshape(-1, model), grad_w_out.astype(BF)])
    attention_flat = lax.psum(attention_flat, "dp")

    bias_parts = grad_bqkv.reshape(3, 2, width)
    mine = jnp.concatenate([bias_parts[0, 0], bias_parts[2, 0], grad_b_up[:hidden_width]])
    theirs = jnp.concatenate([bias_parts[0, 1], bias_parts[2, 1], grad_b_up[hidden_width:]])
    small = lax.psum(mine + inner(theirs), "dp")
    shared = jnp.stack(
        [grad_b_out, grad_gain_one, grad_shift_one, grad_b_down, grad_gain_two, grad_shift_two]
    )
    shared = lax.psum(shared, ("dp", "tensor"))

    gw_qkv = attention_flat[: 3 * width].reshape(model, 3, width).astype(F32)
    return (
        from_sequence(output),
        from_sequence(grad_input),
        gw_qkv[:, 0],
        gw_qkv[:, 1],
        gw_qkv[:, 2],
        small[:width],
        small[width : 2 * width],
        attention_flat[3 * width :].astype(F32),
        shared[0],
        shared[1],
        shared[2],
        feed_flat[:model].astype(F32),
        small[2 * width :],
        feed_flat[model:].astype(F32),
        shared[3],
        shared[4],
        shared[5],
    )


def solution(mesh):
    tokens = P("dp", "tensor", None)
    columns = P(None, "tensor")
    lines = P("tensor", None)
    split = P("tensor")
    whole = P()
    return jax.shard_map(
        shards,
        mesh=mesh,
        in_specs=(tokens, P("dp", None), tokens, columns, columns, columns, split, split, lines)
        + (whole, whole, whole, columns, split, lines, whole, whole, whole),
        out_specs=(tokens, tokens, columns, columns, columns, split, split, lines, whole, whole, whole)
        + (columns, split, lines, whole, whole, whole),
        check_vma=False,
    )
```

```python
import math

import jax
import jax.numpy as jnp
from jax import lax
from jax.sharding import PartitionSpec as P

HEAD_DIM = 64
LAYER_EPSILON = 1e-05
BF = jnp.bfloat16
F32 = jnp.float32


def dot(left, right, contract):
    return lax.dot_general(left, right, (contract, ((), ())), preferred_element_type=F32)


def mm(left, right):
    return dot(left, right, ((1,), (0,)))


def mm_t(left, right):
    return dot(left, right, ((1,), (1,)))


def t_mm(left, right):
    return dot(left, right, ((0,), (0,)))


def normalize(rows):
    centred = rows - jnp.mean(rows, -1, keepdims=True)
    inverse = lax.rsqrt(jnp.mean(centred * centred, -1, keepdims=True) + LAYER_EPSILON)
    return centred * inverse, inverse


def norm_backward(grad, gain, normal, inverse):
    scaled = grad * gain
    mean = jnp.mean(scaled, -1, keepdims=True)
    mean_z = jnp.mean(scaled * normal, -1, keepdims=True)
    return inverse * (scaled - mean - normal * mean_z), jnp.sum(grad * normal, 0), jnp.sum(grad, 0)


def gelu_pair(u):
    root = math.sqrt(2 / math.pi)
    t = jnp.tanh(root * (u + 0.044715 * u * u * u))
    value = 0.5 * u * (1 + t)
    slope = 0.5 * (1 + t) + 0.5 * u * (1 - t * t) * root * (1 + 3 * 0.044715 * u * u)
    return value, slope


def attention_forward(query, keys, values, seg_q, seg_k):
    scores = jnp.einsum("qhd,khd->hqk", query, keys, preferred_element_type=F32) / math.sqrt(HEAD_DIM)
    masked = jnp.where((seg_q[:, None] == seg_k[None, :])[None], scores, -1e30)
    top = jnp.max(masked, -1, keepdims=True)
    exponent = jnp.exp(masked - top)
    total = jnp.sum(exponent, -1, keepdims=True)
    weights = (exponent / total).astype(BF)
    context = jnp.einsum("hqk,khd->qhd", weights, values, preferred_element_type=F32)
    return context.astype(BF), top + jnp.log(total)


def attention_backward(query, keys, values, seg_q, seg_k, logsum, grad):
    scale = 1 / math.sqrt(HEAD_DIM)
    scores = jnp.einsum("qhd,khd->hqk", query, keys, preferred_element_type=F32) * scale
    masked = jnp.where((seg_q[:, None] == seg_k[None, :])[None], scores, -1e30)
    weights = jnp.exp(masked - logsum)
    grad_weights = jnp.einsum("qhd,khd->hqk", grad, values, preferred_element_type=F32)
    row = jnp.sum(weights * grad_weights, -1, keepdims=True)
    grad_scores = (weights * (grad_weights - row)).astype(BF)
    grad_query = jnp.einsum("hqk,khd->qhd", grad_scores, keys, preferred_element_type=F32) * scale
    grad_keys = jnp.einsum("hqk,qhd->khd", grad_scores, query, preferred_element_type=F32) * scale
    grad_values = jnp.einsum("hqk,qhd->khd", weights.astype(BF), grad, preferred_element_type=F32)
    return grad_query.astype(BF), grad_keys, grad_values


def shards(
    inputs,
    segment_ids,
    cotangent,
    w_query,
    w_key,
    w_value,
    b_query,
    b_value,
    w_out,
    b_out,
    gain_one,
    shift_one,
    w_up,
    b_up,
    w_down,
    b_down,
    gain_two,
    shift_two,
):
    ranks = lax.axis_size("tensor")
    rank = lax.axis_index("tensor")
    which = rank % 2
    rows = inputs.shape[1]
    half = 2 * rows
    width = w_query.shape[1]
    hidden_width = w_up.shape[1]
    model = inputs.shape[2]

    def inner(x):
        return lax.ppermute(x, "tensor", [(i, i ^ 1) for i in range(ranks)])

    def outer(x):
        return lax.ppermute(x, "tensor", [(i, i ^ 2) for i in range(ranks)])

    groups = lax.axis_size("dp")
    group = lax.axis_index("dp")

    def across(x, bit):
        return lax.ppermute(x, "dp", [(i, i ^ (1 << bit)) for i in range(groups)])

    def sum_groups(x, order):
        for bit in order:
            low = (group >> bit) % 2 == 0
            part = x.shape[0] // 2
            send = jnp.where(low, x[part:], x[:part]).astype(BF)
            x = jnp.where(low, x[:part], x[part:]) + across(send, bit).astype(F32)
        x = x.astype(BF)
        for bit in reversed(order):
            low = (group >> bit) % 2 == 0
            got = across(x, bit)
            x = jnp.where(low, jnp.concatenate([x, got]), jnp.concatenate([got, x]))
        return x

    def to_sequence(x):
        kept = jnp.where(which == 0, x[0], x[1])
        got = inner(jnp.where(which == 0, x[1], x[0]))
        return jnp.where(which == 0, jnp.concatenate([kept, got]), jnp.concatenate([got, kept]))

    def from_sequence(x):
        low, high = x[:rows], x[rows:]
        kept = jnp.where(which == 0, low, high)
        got = inner(jnp.where(which == 0, high, low))
        return jnp.where(which == 0, jnp.stack([kept, got]), jnp.stack([got, kept]))

    own_in = to_sequence(inputs)
    other_in = outer(own_in)
    own_cot = to_sequence(cotangent).astype(F32)

    def both(x, axis):
        return jnp.concatenate([x, inner(x)], axis)

    wqkv = both(jnp.concatenate([w_query, w_key, w_value], 1)[None], 0)
    wqkv = wqkv.reshape(2, model, 3, width).transpose(1, 2, 0, 3).reshape(model, 3 * 2 * width)
    bias = both(jnp.stack([b_query, b_value])[None], 0).transpose(1, 0, 2).reshape(2, 2 * width)
    bias_qkv = jnp.concatenate([bias[0], jnp.zeros((2 * width,), F32), bias[1]])
    w_out2 = both(w_out, 0)
    w_up2 = both(w_up, 1)
    b_up2 = both(b_up, 0)
    w_down2 = both(w_down, 0)

    segments = jnp.where(which == 0, segment_ids[0], segment_ids[1])
    first = jnp.where(rank // 2 == 0, segments[:half], segments[half:])
    second = jnp.where(rank // 2 == 0, segments[half:], segments[:half])
    seg = jnp.concatenate([first, second])

    heads = 2 * width // HEAD_DIM

    def project(x):
        return (mm(x, wqkv) + bias_qkv).astype(BF)

    qkv = [project(own_in), project(other_in)]

    def split(x):
        return [x[:, i * 2 * width : (i + 1) * 2 * width].reshape(-1, heads, HEAD_DIM) for i in range(3)]

    pieces = [split(x) for x in qkv]
    keys = jnp.concatenate([pieces[0][1], pieces[1][1]])
    values = jnp.concatenate([pieces[0][2], pieces[1][2]])
    context_other, log_other = attention_forward(pieces[1][0], keys, values, second, seg)
    context_other = context_other.reshape(half, 2 * width)
    got = outer(mm(context_other, w_out2).astype(BF))
    context_own, log_own = attention_forward(pieces[0][0], keys, values, first, seg)
    context_own = context_own.reshape(half, 2 * width)
    attended = mm(context_own, w_out2) + got.astype(F32) + b_out
    normal_one, inverse_one = normalize(own_in.astype(F32) + attended)
    hidden_one = normal_one * gain_one + shift_one
    low_own = hidden_one.astype(BF)
    low_other = outer(low_own)

    def feed(low):
        value, slope = gelu_pair(mm(low, w_up2) + b_up2)
        return value.astype(BF), slope

    act_own, slope_own = feed(low_own)
    act_other, slope_other = feed(low_other)
    got = outer(mm(act_other, w_down2).astype(BF))
    branch = mm(act_own, w_down2) + got.astype(F32) + b_down
    normal_two, inverse_two = normalize(hidden_one + branch)
    output = (normal_two * gain_two + shift_two).astype(BF)

    grad_two, grad_gain_two, grad_shift_two = norm_backward(own_cot, gain_two, normal_two, inverse_two)
    gb_own = grad_two.astype(BF)
    grad_b_down = jnp.sum(gb_own.astype(F32), 0)
    gb_other = outer(gb_own)
    before_own = (mm_t(gb_own, w_down2) * slope_own).astype(BF)
    before_other = (mm_t(gb_other, w_down2) * slope_other).astype(BF)
    got = outer(mm_t(before_other, w_up2).astype(BF))
    grad_w_down = t_mm(act_own, gb_own) + t_mm(act_other, gb_other)
    grad_w_up = t_mm(low_own, before_own) + t_mm(low_other, before_other)
    grad_b_up = jnp.sum(before_own.astype(F32), 0) + jnp.sum(before_other.astype(F32), 0)
    grad_hidden = mm_t(before_own, w_up2) + got.astype(F32) + grad_two
    grad_one, grad_gain_one, grad_shift_one = norm_backward(grad_hidden, gain_one, normal_one, inverse_one)
    ga_own = grad_one.astype(BF)
    grad_b_out = jnp.sum(ga_own.astype(F32), 0)
    ga_other = outer(ga_own)

    def pair_sum(mine, theirs):
        return mine + inner(theirs.astype(BF)).astype(F32)

    grad_w_up = pair_sum(grad_w_up[:, :hidden_width], grad_w_up[:, hidden_width:])
    grad_w_down = pair_sum(grad_w_down[:hidden_width], grad_w_down[hidden_width:])
    bits = range(groups.bit_length() - 1)
    orders = (list(bits), list(bits[1:]) + list(bits[:1]))
    grad_w_up = sum_groups(grad_w_up, orders[0])
    grad_w_down = sum_groups(grad_w_down, orders[1])
    shared = jnp.stack(
        [grad_b_out, grad_gain_one, grad_shift_one, grad_b_down, grad_gain_two, grad_shift_two]
    )
    shared = shared + inner(shared)
    shared = shared + outer(shared)

    gc_own = mm_t(ga_own, w_out2).astype(BF)
    gc_other = mm_t(ga_other, w_out2).astype(BF)
    grad_w_out = t_mm(context_own, ga_own) + t_mm(context_other, ga_other)
    shaped = (half, heads, HEAD_DIM)
    gq_own, gk_a, gv_a = attention_backward(
        pieces[0][0], keys, values, first, seg, log_own, gc_own.reshape(shaped)
    )
    gq_other, gk_b, gv_b = attention_backward(
        pieces[1][0], keys, values, second, seg, log_other, gc_other.reshape(shaped)
    )
    flat = (2 * half, 2 * width)
    gk = (gk_a + gk_b).astype(BF).reshape(flat)
    gv = (gv_a + gv_b).astype(BF).reshape(flat)
    gq_own = gq_own.reshape(half, 2 * width)
    gq_other = gq_other.reshape(half, 2 * width)
    gqkv_own = jnp.concatenate([gq_own, gk[:half], gv[:half]], 1)
    gqkv_other = jnp.concatenate([gq_other, gk[half:], gv[half:]], 1)
    got = outer(mm_t(gqkv_other, wqkv).astype(BF))
    grad_wqkv = t_mm(gqkv_own, own_in) + t_mm(gqkv_other, other_in)
    grad_bqkv = jnp.sum(gqkv_own.astype(F32), 0) + jnp.sum(gqkv_other.astype(F32), 0)
    grad_input = mm_t(gqkv_own, wqkv) + got.astype(F32) + grad_one

    by_part = grad_wqkv.reshape(3, 2, width, model)
    mine = jnp.concatenate([by_part[0, 0], by_part[1, 0], by_part[2, 0], grad_w_out[:width]])
    theirs = jnp.concatenate([by_part[0, 1], by_part[1, 1], by_part[2, 1], grad_w_out[width:]])
    grad_attention = pair_sum(mine, theirs)
    grad_attention = jnp.concatenate(
        [
            sum_groups(grad_attention[: 2 * width], orders[0]),
            sum_groups(grad_attention[2 * width :], orders[1]),
        ]
    ).astype(F32)

    bias_parts = grad_bqkv.reshape(3, 2, width)
    mine = jnp.concatenate([bias_parts[0, 0], bias_parts[2, 0], grad_b_up[:hidden_width]])
    theirs = jnp.concatenate([bias_parts[0, 1], bias_parts[2, 1], grad_b_up[hidden_width:]])
    small = jnp.concatenate([shared.reshape(-1), mine + inner(theirs)])
    for bit in bits:
        small = small + across(small, bit)
    shared = small[: 6 * model].reshape(6, model)
    small = small[6 * model :]

    return (
        from_sequence(output),
        from_sequence(grad_input),
        grad_attention[:width].T,
        grad_attention[width : 2 * width].T,
        grad_attention[2 * width : 3 * width].T,
        small[:width],
        small[width : 2 * width],
        grad_attention[3 * width :],
        shared[0],
        shared[1],
        shared[2],
        grad_w_up.astype(F32),
        small[2 * width :],
        grad_w_down.astype(F32),
        shared[3],
        shared[4],
        shared[5],
    )


def solution(mesh):
    tokens = P("dp", "tensor", None)
    columns = P(None, "tensor")
    lines = P("tensor", None)
    split = P("tensor")
    whole = P()
    return jax.shard_map(
        shards,
        mesh=mesh,
        in_specs=(tokens, P("dp", None), tokens, columns, columns, columns, split, split, lines)
        + (whole, whole, whole, columns, split, lines, whole, whole, whole),
        out_specs=(tokens, tokens, columns, columns, columns, split, split, lines, whole, whole, whole)
        + (columns, split, lines, whole, whole, whole),
        check_vma=False,
    )
```

```python
from functools import partial
import math

import jax
import jax.numpy as jnp
from jax import lax
from jax.experimental import pallas as pl
from jax.experimental.pallas import tpu as pltpu
from jax.sharding import PartitionSpec as P

HEAD_DIM = 64
LAYER_EPSILON = 1e-05
BF = jnp.bfloat16
F32 = jnp.float32


def dot(left, right, contract):
    return lax.dot_general(left, right, (contract, ((), ())), preferred_element_type=F32)


def mm(left, right):
    return dot(left, right, ((1,), (0,)))


def mm_t(left, right):
    return dot(left, right, ((1,), (1,)))


def t_mm(left, right):
    return dot(left, right, ((0,), (0,)))


def normalize(rows):
    centred = rows - jnp.mean(rows, -1, keepdims=True)
    inverse = lax.rsqrt(jnp.mean(centred * centred, -1, keepdims=True) + LAYER_EPSILON)
    return centred * inverse, inverse


def norm_backward(grad, gain, normal, inverse):
    scaled = grad * gain
    mean = jnp.mean(scaled, -1, keepdims=True)
    mean_z = jnp.mean(scaled * normal, -1, keepdims=True)
    return inverse * (scaled - mean - normal * mean_z), jnp.sum(grad * normal, 0), jnp.sum(grad, 0)


def gelu_pair(u):
    root = math.sqrt(2 / math.pi)
    t = jnp.tanh(root * (u + 0.044715 * u * u * u))
    value = 0.5 * u * (1 + t)
    slope = 0.5 * (1 + t) + 0.5 * u * (1 - t * t) * root * (1 + 3 * 0.044715 * u * u)
    return value, slope


BLOCK = 256
PAIR = 2 * HEAD_DIM


def block_dot(left, right, contract):
    return lax.dot_general(left, right, (contract, ((), ())), preferred_element_type=F32)


def forward_kernel(flags, qkv, seg_col, seg_row, context, logsum, top, total, acc, *, first, width):
    heads = width // HEAD_DIM
    blocks = qkv.shape[0] // BLOCK
    for q in range(context.shape[0] // BLOCK):
        rows = slice((first + q) * BLOCK, (first + q + 1) * BLOCK)
        top[...] = jnp.full(top.shape, -1e30, F32)
        total[...] = jnp.zeros(total.shape, F32)
        acc[...] = jnp.zeros(acc.shape, F32)
        columns = seg_col[rows, :]

        def step(k, carry):
            @pl.when(flags[(first + q) * blocks + k] > 0)
            def _():
                start = pl.multiple_of(k * BLOCK, BLOCK)
                same = columns == seg_row[k]
                for h in range(heads):
                    at = slice(h * HEAD_DIM, (h + 1) * HEAD_DIM)
                    query = qkv[rows, at] * 0.125
                    keys = qkv[pl.ds(start, BLOCK), width + h * HEAD_DIM : width + (h + 1) * HEAD_DIM]
                    values = qkv[
                        pl.ds(start, BLOCK), 2 * width + h * HEAD_DIM : 2 * width + (h + 1) * HEAD_DIM
                    ]
                    scores = block_dot(query.astype(BF), keys, ((1,), (1,)))
                    scores = jnp.where(same, scores, -1e30)
                    old = top[:, h : h + 1]
                    new = jnp.maximum(old, jnp.max(scores, -1, keepdims=True))
                    weights = jnp.exp(scores - new)
                    decay = jnp.exp(old - new)
                    top[:, h : h + 1] = new
                    total[:, h : h + 1] = total[:, h : h + 1] * decay + jnp.sum(weights, -1, keepdims=True)
                    acc[:, at] = acc[:, at] * decay + block_dot(weights.astype(BF), values, ((1,), (0,)))

            return carry

        lax.fori_loop(0, blocks, step, 0)
        out = slice(q * BLOCK, (q + 1) * BLOCK)
        for h in range(heads):
            at = slice(h * HEAD_DIM, (h + 1) * HEAD_DIM)
            context[out, at] = (acc[:, at] / total[:, h : h + 1]).astype(BF)
        logs = top[:, :heads] + jnp.log(total[:, :heads])
        for h in range(heads):
            top[:, h : h + 1] = logs[:, h : h + 1]
        logsum[:, out] = top[...].T[:8]


def backward_kernel(
    flags, qkv_q, qkv_k, qkv_v, seg_col, seg_row, log_a, log_b, ctx_a, ctx_b, gc_a, gc_b, grad, acc, delta, logs, gc, *, first
):
    width = qkv_q.shape[1]
    heads = width // HEAD_DIM
    blocks = qkv_q.shape[0] // BLOCK
    half = ctx_a.shape[0]
    acc[...] = jnp.zeros(acc.shape, F32)
    pick = lax.broadcasted_iota(jnp.int32, (8, width), 1) // HEAD_DIM
    pick = (pick == lax.broadcasted_iota(jnp.int32, (8, width), 0)).astype(F32)
    for index, (log, ctx, source) in enumerate(((log_a, ctx_a, gc_a), (log_b, ctx_b, gc_b))):
        gc[index * half : (index + 1) * half, :] = source[...]
        for part in range(half // BLOCK):
            at = slice(part * BLOCK, (part + 1) * BLOCK)
            product = source[at, :].astype(F32) * ctx[at, :].astype(F32)
            row = lax.dot_general(
                pick, product, (((1,), (1,)), ((), ())), precision=lax.Precision.HIGHEST, preferred_element_type=F32
            )
            delta[index * (half // BLOCK) + part] = row
            logs[index * (half // BLOCK) + part] = log[:, at]

    def step(pair, carry):
        k = pair // blocks
        q = pair % blocks

        @pl.when(flags[pair] > 0)
        def _():
            key_rows = pl.ds(pl.multiple_of(k * BLOCK, BLOCK), BLOCK)
            query_rows = pl.ds(pl.multiple_of(q * BLOCK, BLOCK), BLOCK)
            same = seg_col[key_rows, :] == seg_row[q]
            log_rows = logs[q]
            delta_rows = delta[q]
            for h in range(heads):
                at_q = slice(h * HEAD_DIM, (h + 1) * HEAD_DIM)
                at_k = slice(width + h * HEAD_DIM, width + (h + 1) * HEAD_DIM)
                at_v = slice(2 * width + h * HEAD_DIM, 2 * width + (h + 1) * HEAD_DIM)
                query = (qkv_q[query_rows, at_q] * 0.125).astype(BF)
                keys = qkv_k[key_rows, at_q]
                out = gc[query_rows, at_q]
                scores = block_dot(keys, query, ((1,), (1,)))
                weights = jnp.where(same, jnp.exp(jnp.where(same, scores, -1e30) - log_rows[first + h : first + h + 1, :]), 0.0)
                grad_weights = block_dot(qkv_v[key_rows, at_q], out, ((1,), (1,)))
                grad_scores = (weights * (grad_weights - delta_rows[h : h + 1, :])).astype(BF)
                acc[key_rows, at_v] += block_dot(weights.astype(BF), out, ((1,), (0,)))
                acc[key_rows, at_k] += block_dot(grad_scores, query, ((1,), (0,)))
                acc[query_rows, at_q] += block_dot(grad_scores, keys, ((0,), (0,)))

        return carry

    lax.fori_loop(0, blocks * blocks, step, 0)
    grad[:, :width] = (acc[:, :width] * 0.125).astype(BF)
    grad[:, width:] = acc[:, width:].astype(BF)


def attention_forward(flags, qkv, seg_col, seg_row, index, width):
    half = qkv.shape[0] // 2
    return pl.pallas_call(
        partial(forward_kernel, first=index * (half // BLOCK), width=width),
        out_shape=(jax.ShapeDtypeStruct((half, width), BF), jax.ShapeDtypeStruct((8, half), F32)),
        in_specs=[pl.BlockSpec(memory_space=pltpu.SMEM)] + [pl.BlockSpec(memory_space=pltpu.VMEM)] * 3,
        scratch_shapes=[
            pltpu.VMEM((BLOCK, 128), F32),
            pltpu.VMEM((BLOCK, 128), F32),
            pltpu.VMEM((BLOCK, width), F32),
        ],
        cost_estimate=pl.CostEstimate(flops=3 * 10**9, transcendentals=3 * 10**6, bytes_accessed=4 * 10**6),
        name="attention_forward",
    )(flags, qkv, seg_col, seg_row)


def attention_backward(flags, qkv, seg_col, seg_row, logs, contexts, grads, index, width):
    tokens = qkv.shape[0]
    half = tokens // 2
    count = width // PAIR
    whole = pl.BlockSpec(memory_space=pltpu.VMEM)

    def part(rows, at):
        return pl.BlockSpec((rows, PAIR), lambda i: (0, at))

    return pl.pallas_call(
        partial(backward_kernel, first=index * (PAIR // HEAD_DIM)),
        grid=(1,),
        out_shape=jax.ShapeDtypeStruct((tokens, 3 * PAIR), BF),
        in_specs=[pl.BlockSpec(memory_space=pltpu.SMEM)]
        + [part(tokens, index + count * i) for i in range(3)]
        + [whole] * 4
        + [part(half, index)] * 4,
        out_specs=pl.BlockSpec((tokens, 3 * PAIR), lambda i: (0, 0)),
        scratch_shapes=[
            pltpu.VMEM((tokens, 3 * PAIR), F32),
            pltpu.VMEM((tokens // BLOCK, 8, BLOCK), F32),
            pltpu.VMEM((tokens // BLOCK, 8, BLOCK), F32),
            pltpu.VMEM((tokens, PAIR), BF),
        ],
        cost_estimate=pl.CostEstimate(flops=5 * 10**9, transcendentals=2 * 10**6, bytes_accessed=4 * 10**6),
        name=f"attention_backward_{index}",
    )(flags, qkv, qkv, qkv, seg_col, seg_row, *logs, *contexts, *grads)


def shards(
    inputs,
    segment_ids,
    cotangent,
    w_query,
    w_key,
    w_value,
    b_query,
    b_value,
    w_out,
    b_out,
    gain_one,
    shift_one,
    w_up,
    b_up,
    w_down,
    b_down,
    gain_two,
    shift_two,
):
    ranks = lax.axis_size("tensor")
    rank = lax.axis_index("tensor")
    which = rank % 2
    rows = inputs.shape[1]
    half = 2 * rows
    width = w_query.shape[1]
    hidden_width = w_up.shape[1]
    model = inputs.shape[2]

    def inner(x):
        return lax.ppermute(x, "tensor", [(i, i ^ 1) for i in range(ranks)])

    def outer(x):
        return lax.ppermute(x, "tensor", [(i, i ^ 2) for i in range(ranks)])

    groups = lax.axis_size("dp")
    group = lax.axis_index("dp")

    def across(x, bit):
        return lax.ppermute(x, "dp", [(i, i ^ (1 << bit)) for i in range(groups)])

    def sum_steps(x, order):
        for bit in order:
            low = (group >> bit) % 2 == 0
            part = x.shape[0] // 2
            send = jnp.where(low, x[part:], x[:part]).astype(BF)
            x = jnp.where(low, x[:part], x[part:]) + across(send, bit).astype(F32)
            yield x
        x = x.astype(BF)
        for bit in reversed(order):
            low = (group >> bit) % 2 == 0
            got = across(x, bit)
            x = jnp.where(low, jnp.concatenate([x, got]), jnp.concatenate([got, x]))
            yield x

    def advance(steps, keep, times=1):
        for _ in range(times):
            value = next(steps, None)
            if value is not None:
                keep = [value]
        return keep

    def finish(steps, keep):
        for value in steps:
            keep = [value]
        return keep[0]

    def to_sequence(x):
        kept = jnp.where(which == 0, x[0], x[1])
        got = inner(jnp.where(which == 0, x[1], x[0]))
        return jnp.where(which == 0, jnp.concatenate([kept, got]), jnp.concatenate([got, kept]))

    def from_sequence(x):
        low, high = x[:rows], x[rows:]
        kept = jnp.where(which == 0, low, high)
        got = inner(jnp.where(which == 0, high, low))
        return jnp.where(which == 0, jnp.stack([kept, got]), jnp.stack([got, kept]))

    own_in = to_sequence(inputs)
    other_in = outer(own_in)
    own_cot = to_sequence(cotangent).astype(F32)

    def both(x, axis):
        return jnp.concatenate([x, inner(x)], axis)

    wqkv = both(jnp.concatenate([w_query, w_key, w_value], 1)[None], 0)
    wqkv = wqkv.reshape(2, model, 3, width).transpose(1, 2, 0, 3).reshape(model, 3 * 2 * width)
    bias = both(jnp.stack([b_query, b_value])[None], 0).transpose(1, 0, 2).reshape(2, 2 * width)
    bias_qkv = jnp.concatenate([bias[0], jnp.zeros((2 * width,), F32), bias[1]])
    w_out2 = both(w_out, 0)
    w_up2 = both(w_up, 1)
    b_up2 = both(b_up, 0)
    w_down2 = both(w_down, 0)

    segments = jnp.where(which == 0, segment_ids[0], segment_ids[1])
    first = jnp.where(rank // 2 == 0, segments[:half], segments[half:])
    second = jnp.where(rank // 2 == 0, segments[half:], segments[:half])
    seg = jnp.concatenate([first, second])

    blocked = seg.reshape(-1, BLOCK)
    low_id, high_id = blocked[:, 0], blocked[:, -1]
    flags = (low_id[:, None] <= high_id[None, :]) & (low_id[None, :] <= high_id[:, None])
    flags = flags.astype(jnp.int32).reshape(-1)
    seg_col = seg[:, None]
    seg_row = seg.reshape(-1, 1, BLOCK)

    def project(x):
        return (mm(x, wqkv) + bias_qkv).astype(BF)

    qkv = jnp.concatenate([project(own_in), project(other_in)])
    context_other, log_other = attention_forward(flags, qkv, seg_col, seg_row, 1, 2 * width)
    got = outer(mm(context_other, w_out2).astype(BF))
    context_own, log_own = attention_forward(flags, qkv, seg_col, seg_row, 0, 2 * width)
    attended = mm(context_own, w_out2) + got.astype(F32) + b_out
    normal_one, inverse_one = normalize(own_in.astype(F32) + attended)
    hidden_one = normal_one * gain_one + shift_one
    low_own = hidden_one.astype(BF)
    low_other = outer(low_own)

    def feed(low):
        value, slope = gelu_pair(mm(low, w_up2) + b_up2)
        return value.astype(BF), slope

    act_own, slope_own = feed(low_own)
    act_other, slope_other = feed(low_other)
    got = outer(mm(act_other, w_down2).astype(BF))
    branch = mm(act_own, w_down2) + got.astype(F32) + b_down
    normal_two, inverse_two = normalize(hidden_one + branch)
    output = (normal_two * gain_two + shift_two).astype(BF)

    grad_two, grad_gain_two, grad_shift_two = norm_backward(own_cot, gain_two, normal_two, inverse_two)
    gb_own = grad_two.astype(BF)
    grad_b_down = jnp.sum(gb_own.astype(F32), 0)
    gb_other = outer(gb_own)
    before_own = (mm_t(gb_own, w_down2) * slope_own).astype(BF)
    before_other = (mm_t(gb_other, w_down2) * slope_other).astype(BF)
    got = outer(mm_t(before_other, w_up2).astype(BF))
    grad_w_down = t_mm(act_own, gb_own) + t_mm(act_other, gb_other)
    grad_w_up = t_mm(low_own, before_own) + t_mm(low_other, before_other)
    grad_b_up = jnp.sum(before_own.astype(F32), 0) + jnp.sum(before_other.astype(F32), 0)
    grad_hidden = mm_t(before_own, w_up2) + got.astype(F32) + grad_two
    grad_one, grad_gain_one, grad_shift_one = norm_backward(grad_hidden, gain_one, normal_one, inverse_one)
    ga_own = grad_one.astype(BF)
    grad_b_out = jnp.sum(ga_own.astype(F32), 0)
    ga_other = outer(ga_own)

    def pair_sum(mine, theirs):
        return mine + inner(theirs.astype(BF)).astype(F32)

    grad_w_up = pair_sum(grad_w_up[:, :hidden_width], grad_w_up[:, hidden_width:])
    grad_w_down = pair_sum(grad_w_down[:hidden_width], grad_w_down[hidden_width:])
    bits = range(groups.bit_length() - 1)
    orders = (list(bits), list(bits[1:]) + list(bits[:1]))
    up_steps, down_steps = sum_steps(grad_w_up, orders[0]), sum_steps(grad_w_down, orders[1])
    up_now, down_now = advance(up_steps, None), advance(down_steps, None)
    shared = jnp.stack(
        [grad_b_out, grad_gain_one, grad_shift_one, grad_b_down, grad_gain_two, grad_shift_two]
    )
    shared = shared + inner(shared)
    shared = shared + outer(shared)

    gc_own = mm_t(ga_own, w_out2).astype(BF)
    gc_other = mm_t(ga_other, w_out2).astype(BF)
    grad_w_out = t_mm(context_own, ga_own) + t_mm(context_other, ga_other)
    pairs = []
    for index in range(2 * width // PAIR):
        tied = lax.optimization_barrier((flags, up_now[0], down_now[0]))
        pairs.append(
            attention_backward(
                tied[0],
                qkv,
                seg_col,
                seg_row,
                (log_own, log_other),
                (context_own, context_other),
                (gc_own, gc_other),
                index,
                2 * width,
            )
        )
        up_now, down_now = advance(up_steps, up_now), advance(down_steps, down_now)
    gqkv = jnp.concatenate([x[:, i * PAIR : (i + 1) * PAIR] for i in range(3) for x in pairs], 1)
    tied = lax.optimization_barrier((gqkv, up_now[0], down_now[0]))
    gqkv = tied[0]
    grad_w_up, grad_w_down = finish(up_steps, up_now), finish(down_steps, down_now)
    gqkv_own, gqkv_other = gqkv[:half], gqkv[half:]
    got = outer(mm_t(gqkv_other, wqkv).astype(BF))
    grad_wqkv = t_mm(gqkv_own, own_in) + t_mm(gqkv_other, other_in)
    grad_bqkv = jnp.sum(gqkv_own.astype(F32), 0) + jnp.sum(gqkv_other.astype(F32), 0)
    grad_input = mm_t(gqkv_own, wqkv) + got.astype(F32) + grad_one

    by_part = grad_wqkv.reshape(3, 2, width, model)
    mine = jnp.concatenate([by_part[0, 0], by_part[1, 0], by_part[2, 0], grad_w_out[:width]])
    theirs = jnp.concatenate([by_part[0, 1], by_part[1, 1], by_part[2, 1], grad_w_out[width:]])
    grad_attention = pair_sum(mine, theirs)
    grad_attention = jnp.concatenate(
        [
            finish(sum_steps(grad_attention[: 2 * width], orders[0]), None),
            finish(sum_steps(grad_attention[2 * width :], orders[1]), None),
        ]
    ).astype(F32)

    bias_parts = grad_bqkv.reshape(3, 2, width)
    mine = jnp.concatenate([bias_parts[0, 0], bias_parts[2, 0], grad_b_up[:hidden_width]])
    theirs = jnp.concatenate([bias_parts[0, 1], bias_parts[2, 1], grad_b_up[hidden_width:]])
    small = jnp.concatenate([shared.reshape(-1), mine + inner(theirs)])
    for bit in bits:
        small = small + across(small, bit)
    shared = small[: 6 * model].reshape(6, model)
    small = small[6 * model :]

    return (
        from_sequence(output),
        from_sequence(grad_input),
        grad_attention[:width].T,
        grad_attention[width : 2 * width].T,
        grad_attention[2 * width : 3 * width].T,
        small[:width],
        small[width : 2 * width],
        grad_attention[3 * width :],
        shared[0],
        shared[1],
        shared[2],
        grad_w_up.astype(F32),
        small[2 * width :],
        grad_w_down.astype(F32),
        shared[3],
        shared[4],
        shared[5],
    )


def solution(mesh):
    tokens = P("dp", "tensor", None)
    columns = P(None, "tensor")
    lines = P("tensor", None)
    split = P("tensor")
    whole = P()
    return jax.shard_map(
        shards,
        mesh=mesh,
        in_specs=(tokens, P("dp", None), tokens, columns, columns, columns, split, split, lines)
        + (whole, whole, whole, columns, split, lines, whole, whole, whole),
        out_specs=(tokens, tokens, columns, columns, columns, split, split, lines, whole, whole, whole)
        + (columns, split, lines, whole, whole, whole),
        check_vma=False,
    )
```

```python
from functools import partial
import math

import jax
import jax.numpy as jnp
from jax import lax
from jax.experimental import pallas as pl
from jax.experimental.pallas import tpu as pltpu
from jax.sharding import PartitionSpec as P

HEAD_DIM = 64
LAYER_EPSILON = 1e-05
BF = jnp.bfloat16
F32 = jnp.float32


def dot(left, right, contract):
    return lax.dot_general(left, right, (contract, ((), ())), preferred_element_type=F32)


def mm(left, right):
    return dot(left, right, ((1,), (0,)))


def mm_t(left, right):
    return dot(left, right, ((1,), (1,)))


def t_mm(left, right):
    return dot(left, right, ((0,), (0,)))


def normalize(rows):
    centred = rows - jnp.mean(rows, -1, keepdims=True)
    inverse = lax.rsqrt(jnp.mean(centred * centred, -1, keepdims=True) + LAYER_EPSILON)
    return centred * inverse, inverse


def norm_backward(grad, gain, normal, inverse):
    scaled = grad * gain
    mean = jnp.mean(scaled, -1, keepdims=True)
    mean_z = jnp.mean(scaled * normal, -1, keepdims=True)
    return inverse * (scaled - mean - normal * mean_z), jnp.sum(grad * normal, 0), jnp.sum(grad, 0)


def gelu_pair(u):
    root = math.sqrt(2 / math.pi)
    t = jnp.tanh(root * (u + 0.044715 * u * u * u))
    value = 0.5 * u * (1 + t)
    slope = 0.5 * (1 + t) + 0.5 * u * (1 - t * t) * root * (1 + 3 * 0.044715 * u * u)
    return value, slope


BLOCK = 256


def block_dot(left, right, contract):
    return lax.dot_general(left, right, (contract, ((), ())), preferred_element_type=F32)


def forward_kernel(flags, qkv, seg_col, seg_row, context, logsum, top, total, acc, *, first, width):
    heads = width // HEAD_DIM
    blocks = qkv.shape[0] // BLOCK
    logsum[...] = jnp.zeros(logsum.shape, F32)
    for q in range(context.shape[0] // BLOCK):
        rows = slice((first + q) * BLOCK, (first + q + 1) * BLOCK)
        top[...] = jnp.full(top.shape, -1e30, F32)
        total[...] = jnp.zeros(total.shape, F32)
        acc[...] = jnp.zeros(acc.shape, F32)
        columns = seg_row[first + q]

        def step(k, carry):
            @pl.when(flags[(first + q) * blocks + k] > 0)
            def _():
                keys_at = pl.ds(pl.multiple_of(k * BLOCK, BLOCK), BLOCK)
                same = seg_col[keys_at, :] == columns
                for h in range(heads):
                    at = slice(h * HEAD_DIM, (h + 1) * HEAD_DIM)
                    query = (qkv[rows, at] * 0.125).astype(BF)
                    keys = qkv[keys_at, width + h * HEAD_DIM : width + (h + 1) * HEAD_DIM]
                    values = qkv[keys_at, 2 * width + h * HEAD_DIM : 2 * width + (h + 1) * HEAD_DIM]
                    scores = jnp.where(same, block_dot(keys, query, ((1,), (1,))), -1e30)
                    old = top[h : h + 1, :]
                    new = jnp.maximum(old, jnp.max(scores, 0, keepdims=True))
                    weights = jnp.exp(scores - new)
                    decay = jnp.exp(old - new)
                    top[h : h + 1, :] = new
                    total[h : h + 1, :] = total[h : h + 1, :] * decay + jnp.sum(weights, 0, keepdims=True)
                    acc[at, :] = acc[at, :] * decay + block_dot(values, weights.astype(BF), ((0,), (0,)))

            return carry

        lax.fori_loop(0, blocks, step, 0)
        out = slice(q * BLOCK, (q + 1) * BLOCK)
        for h in range(heads):
            at = slice(h * HEAD_DIM, (h + 1) * HEAD_DIM)
            acc[at, :] = acc[at, :] / total[h : h + 1, :]
            logsum[h : h + 1, out] = top[h : h + 1, :] + jnp.log(total[h : h + 1, :])
        context[out, :] = acc[...].T.astype(BF)


def backward_kernel(
    flags, qkv_q, qkv_k, qkv_v, seg_col, seg_row, log_a, log_b, ctx_a, ctx_b, gc_a, gc_b, grad, acc, delta, logs, gc, *, first
):
    width = qkv_q.shape[1]
    heads = width // HEAD_DIM
    blocks = qkv_q.shape[0] // BLOCK
    half = ctx_a.shape[0]
    acc[...] = jnp.zeros(acc.shape, F32)
    pick = lax.broadcasted_iota(jnp.int32, (8, width), 1) // HEAD_DIM
    pick = (pick == lax.broadcasted_iota(jnp.int32, (8, width), 0)).astype(F32)
    for index, (log, ctx, source) in enumerate(((log_a, ctx_a, gc_a), (log_b, ctx_b, gc_b))):
        gc[index * half : (index + 1) * half, :] = source[...]
        for part in range(half // BLOCK):
            at = slice(part * BLOCK, (part + 1) * BLOCK)
            product = source[at, :].astype(F32) * ctx[at, :].astype(F32)
            row = lax.dot_general(
                pick, product, (((1,), (1,)), ((), ())), precision=lax.Precision.HIGHEST, preferred_element_type=F32
            )
            delta[index * (half // BLOCK) + part] = row
            logs[index * (half // BLOCK) + part] = log[:, at]

    def step(pair, carry):
        k = pair // blocks
        q = pair % blocks

        @pl.when(flags[pair] > 0)
        def _():
            key_rows = pl.ds(pl.multiple_of(k * BLOCK, BLOCK), BLOCK)
            query_rows = pl.ds(pl.multiple_of(q * BLOCK, BLOCK), BLOCK)
            same = seg_col[key_rows, :] == seg_row[q]
            log_rows = logs[q]
            delta_rows = delta[q]
            for h in range(heads):
                at_q = slice(h * HEAD_DIM, (h + 1) * HEAD_DIM)
                at_k = slice(width + h * HEAD_DIM, width + (h + 1) * HEAD_DIM)
                at_v = slice(2 * width + h * HEAD_DIM, 2 * width + (h + 1) * HEAD_DIM)
                query = (qkv_q[query_rows, at_q] * 0.125).astype(BF)
                keys = qkv_k[key_rows, at_q]
                out = gc[query_rows, at_q]
                scores = block_dot(keys, query, ((1,), (1,)))
                weights = jnp.where(same, jnp.exp(jnp.where(same, scores, -1e30) - log_rows[first + h : first + h + 1, :]), 0.0)
                grad_weights = block_dot(qkv_v[key_rows, at_q], out, ((1,), (1,)))
                grad_scores = (weights * (grad_weights - delta_rows[h : h + 1, :])).astype(BF)
                acc[key_rows, at_v] += block_dot(weights.astype(BF), out, ((1,), (0,)))
                acc[key_rows, at_k] += block_dot(grad_scores, query, ((1,), (0,)))
                acc[query_rows, at_q] += block_dot(grad_scores, keys, ((0,), (0,)))

        return carry

    lax.fori_loop(0, blocks * blocks, step, 0)
    grad[:, :width] = (acc[:, :width] * 0.125).astype(BF)
    grad[:, width:] = acc[:, width:].astype(BF)


def attention_forward(flags, qkv, seg_col, seg_row, index, width):
    half = qkv.shape[0] // 2
    return pl.pallas_call(
        partial(forward_kernel, first=index * (half // BLOCK), width=width),
        out_shape=(jax.ShapeDtypeStruct((half, width), BF), jax.ShapeDtypeStruct((8, half), F32)),
        in_specs=[pl.BlockSpec(memory_space=pltpu.SMEM)] + [pl.BlockSpec(memory_space=pltpu.VMEM)] * 3,
        scratch_shapes=[
            pltpu.VMEM((8, BLOCK), F32),
            pltpu.VMEM((8, BLOCK), F32),
            pltpu.VMEM((width, BLOCK), F32),
        ],
        cost_estimate=pl.CostEstimate(flops=3 * 10**9, transcendentals=3 * 10**6, bytes_accessed=4 * 10**6),
        name="attention_forward",
    )(flags, qkv, seg_col, seg_row)


def attention_backward(flags, qkv, seg_col, seg_row, logs, contexts, grads, width):
    tokens = qkv.shape[0]
    half = tokens // 2
    index, count = 0, 1
    whole = pl.BlockSpec(memory_space=pltpu.VMEM)

    def part(rows, at):
        return pl.BlockSpec((rows, width), lambda i: (0, at))

    return pl.pallas_call(
        partial(backward_kernel, first=index * (width // HEAD_DIM)),
        grid=(1,),
        out_shape=jax.ShapeDtypeStruct((tokens, 3 * width), BF),
        in_specs=[pl.BlockSpec(memory_space=pltpu.SMEM)]
        + [part(tokens, index + count * i) for i in range(3)]
        + [whole] * 4
        + [part(half, index)] * 4,
        out_specs=pl.BlockSpec((tokens, 3 * width), lambda i: (0, 0)),
        scratch_shapes=[
            pltpu.VMEM((tokens, 3 * width), F32),
            pltpu.VMEM((tokens // BLOCK, 8, BLOCK), F32),
            pltpu.VMEM((tokens // BLOCK, 8, BLOCK), F32),
            pltpu.VMEM((tokens, width), BF),
        ],
        cost_estimate=pl.CostEstimate(flops=15 * 10**9, transcendentals=6 * 10**6, bytes_accessed=4 * 10**6),
        name="attention_backward",
    )(flags, qkv, qkv, qkv, seg_col, seg_row, *logs, *contexts, *grads)


def shards(
    inputs,
    segment_ids,
    cotangent,
    w_query,
    w_key,
    w_value,
    b_query,
    b_value,
    w_out,
    b_out,
    gain_one,
    shift_one,
    w_up,
    b_up,
    w_down,
    b_down,
    gain_two,
    shift_two,
):
    ranks = lax.axis_size("tensor")
    rank = lax.axis_index("tensor")
    which = rank % 2
    rows = inputs.shape[1]
    half = 2 * rows
    width = w_query.shape[1]
    hidden_width = w_up.shape[1]
    model = inputs.shape[2]

    def inner(x):
        return lax.ppermute(x, "tensor", [(i, i ^ 1) for i in range(ranks)])

    def outer(x):
        return lax.ppermute(x, "tensor", [(i, i ^ 2) for i in range(ranks)])

    groups = lax.axis_size("dp")
    group = lax.axis_index("dp")

    def across(x, mask):
        return lax.ppermute(x, "dp", [(i, i ^ mask) for i in range(groups)])

    def sum_groups(x, order):
        for shift, count in order:
            own = (group >> shift) % count
            part = x.shape[0] // count
            total = lax.dynamic_slice_in_dim(x, own * part, part)
            for j in range(1, count):
                send = lax.dynamic_slice_in_dim(x, (own ^ j) * part, part).astype(BF)
                total = total + across(send, j << shift).astype(F32)
            x = total
        x = x.astype(BF)
        for shift, count in reversed(order):
            own = (group >> shift) % count
            part = x.shape[0]
            whole = jnp.zeros((part * count,) + x.shape[1:], BF)
            whole = lax.dynamic_update_slice_in_dim(whole, x, own * part, 0)
            for j in range(1, count):
                whole = lax.dynamic_update_slice_in_dim(whole, across(x, j << shift), (own ^ j) * part, 0)
            x = whole
        return x

    def to_sequence(x):
        kept = jnp.where(which == 0, x[0], x[1])
        got = inner(jnp.where(which == 0, x[1], x[0]))
        return jnp.where(which == 0, jnp.concatenate([kept, got]), jnp.concatenate([got, kept]))

    def from_sequence(x):
        low, high = x[:rows], x[rows:]
        kept = jnp.where(which == 0, low, high)
        got = inner(jnp.where(which == 0, high, low))
        return jnp.where(which == 0, jnp.stack([kept, got]), jnp.stack([got, kept]))

    own_in = to_sequence(inputs)
    other_in = outer(own_in)
    own_cot = to_sequence(cotangent).astype(F32)

    def both(x, axis):
        return jnp.concatenate([x, inner(x)], axis)

    wqkv = both(jnp.concatenate([w_query, w_key, w_value], 1)[None], 0)
    wqkv = wqkv.reshape(2, model, 3, width).transpose(1, 2, 0, 3).reshape(model, 3 * 2 * width)
    bias = both(jnp.stack([b_query, b_value])[None], 0).transpose(1, 0, 2).reshape(2, 2 * width)
    bias_qkv = jnp.concatenate([bias[0], jnp.zeros((2 * width,), F32), bias[1]])
    w_out2 = both(w_out, 0)
    w_up2 = both(w_up, 1)
    b_up2 = both(b_up, 0)
    w_down2 = both(w_down, 0)

    segments = jnp.where(which == 0, segment_ids[0], segment_ids[1])
    first = jnp.where(rank // 2 == 0, segments[:half], segments[half:])
    second = jnp.where(rank // 2 == 0, segments[half:], segments[:half])
    seg = jnp.concatenate([first, second])

    blocked = seg.reshape(-1, BLOCK)
    low_id, high_id = blocked[:, 0], blocked[:, -1]
    flags = (low_id[:, None] <= high_id[None, :]) & (low_id[None, :] <= high_id[:, None])
    flags = flags.astype(jnp.int32).reshape(-1)
    seg_col = seg[:, None]
    seg_row = seg.reshape(-1, 1, BLOCK)

    def project(x):
        return (mm(x, wqkv) + bias_qkv).astype(BF)

    qkv = jnp.concatenate([project(own_in), project(other_in)])
    context_other, log_other = attention_forward(flags, qkv, seg_col, seg_row, 1, 2 * width)
    got = outer(mm(context_other, w_out2).astype(BF))
    context_own, log_own = attention_forward(flags, qkv, seg_col, seg_row, 0, 2 * width)
    attended = mm(context_own, w_out2) + got.astype(F32) + b_out
    normal_one, inverse_one = normalize(own_in.astype(F32) + attended)
    hidden_one = normal_one * gain_one + shift_one
    low_own = hidden_one.astype(BF)
    low_other = outer(low_own)

    def feed(low):
        value, slope = gelu_pair(mm(low, w_up2) + b_up2)
        return value.astype(BF), slope

    act_own, slope_own = feed(low_own)
    act_other, slope_other = feed(low_other)
    got = outer(mm(act_other, w_down2).astype(BF))
    branch = mm(act_own, w_down2) + got.astype(F32) + b_down
    normal_two, inverse_two = normalize(hidden_one + branch)
    output = (normal_two * gain_two + shift_two).astype(BF)

    grad_two, grad_gain_two, grad_shift_two = norm_backward(own_cot, gain_two, normal_two, inverse_two)
    gb_own = grad_two.astype(BF)
    grad_b_down = jnp.sum(gb_own.astype(F32), 0)
    gb_other = outer(gb_own)
    before_own = (mm_t(gb_own, w_down2) * slope_own).astype(BF)
    before_other = (mm_t(gb_other, w_down2) * slope_other).astype(BF)
    got = outer(mm_t(before_other, w_up2).astype(BF))
    grad_w_down = t_mm(act_own, gb_own) + t_mm(act_other, gb_other)
    grad_w_up = t_mm(low_own, before_own) + t_mm(low_other, before_other)
    grad_b_up = jnp.sum(before_own.astype(F32), 0) + jnp.sum(before_other.astype(F32), 0)
    grad_hidden = mm_t(before_own, w_up2) + got.astype(F32) + grad_two
    grad_one, grad_gain_one, grad_shift_one = norm_backward(grad_hidden, gain_one, normal_one, inverse_one)
    ga_own = grad_one.astype(BF)
    grad_b_out = jnp.sum(ga_own.astype(F32), 0)
    ga_other = outer(ga_own)

    def pair_sum(mine, theirs):
        return mine + inner(theirs.astype(BF)).astype(F32)

    grad_w_up = pair_sum(grad_w_up[:, :hidden_width], grad_w_up[:, hidden_width:])
    grad_w_down = pair_sum(grad_w_down[:hidden_width], grad_w_down[hidden_width:])
    grad_w_out = t_mm(context_own, ga_own) + t_mm(context_other, ga_other)
    grad_w_out = pair_sum(grad_w_out[:width], grad_w_out[width:])
    summed = (grad_w_up.astype(BF), grad_w_down.astype(BF), grad_w_out.astype(BF))
    flags, summed = lax.optimization_barrier((flags, summed))
    grad_w_up, grad_w_down, grad_w_out = lax.psum(summed, "dp")
    order = [(0, 2)] + [(i, min(4, groups >> i)) for i in range(1, groups.bit_length() - 1, 2)]
    orders = (order, order[::-1])

    gc_own = mm_t(ga_own, w_out2).astype(BF)
    gc_other = mm_t(ga_other, w_out2).astype(BF)
    gqkv = attention_backward(
        flags, qkv, seg_col, seg_row, (log_own, log_other), (context_own, context_other), (gc_own, gc_other), 2 * width
    )
    gqkv_own, gqkv_other = gqkv[:half], gqkv[half:]
    got = outer(mm_t(gqkv_other, wqkv).astype(BF))
    grad_wqkv = t_mm(gqkv_own, own_in) + t_mm(gqkv_other, other_in)
    grad_bqkv = jnp.sum(gqkv_own.astype(F32), 0) + jnp.sum(gqkv_other.astype(F32), 0)
    grad_input = mm_t(gqkv_own, wqkv) + got.astype(F32) + grad_one

    by_part = grad_wqkv.reshape(3, 2, width, model)
    grad_qkv = pair_sum(by_part[:, 0].reshape(3 * width, model), by_part[:, 1].reshape(3 * width, model))
    cut = 3 * width // groups // 2 * groups
    grad_qkv = jnp.concatenate([sum_groups(grad_qkv[:cut], orders[0]), sum_groups(grad_qkv[cut:], orders[1])])
    grad_qkv = grad_qkv.astype(F32)

    shared = jnp.stack(
        [grad_b_out, grad_gain_one, grad_shift_one, grad_b_down, grad_gain_two, grad_shift_two]
    )
    shared = lax.optimization_barrier((shared, gqkv_other))[0]
    shared = shared + inner(shared)
    shared = shared + outer(shared)
    bias_parts = grad_bqkv.reshape(3, 2, width)
    mine = jnp.concatenate([bias_parts[0, 0], bias_parts[2, 0], grad_b_up[:hidden_width]])
    theirs = jnp.concatenate([bias_parts[0, 1], bias_parts[2, 1], grad_b_up[hidden_width:]])
    small = jnp.concatenate([shared.reshape(-1), mine + inner(theirs)])
    for bit in range(groups.bit_length() - 1):
        small = small + across(small, 1 << bit)
    shared = small[: 6 * model].reshape(6, model)
    small = small[6 * model :]

    return (
        from_sequence(output),
        from_sequence(grad_input),
        grad_qkv[:width].T,
        grad_qkv[width : 2 * width].T,
        grad_qkv[2 * width : 3 * width].T,
        small[:width],
        small[width : 2 * width],
        grad_w_out.astype(F32),
        shared[0],
        shared[1],
        shared[2],
        grad_w_up.astype(F32),
        small[2 * width :],
        grad_w_down.astype(F32),
        shared[3],
        shared[4],
        shared[5],
    )


def solution(mesh):
    tokens = P("dp", "tensor", None)
    columns = P(None, "tensor")
    lines = P("tensor", None)
    split = P("tensor")
    whole = P()
    return jax.shard_map(
        shards,
        mesh=mesh,
        in_specs=(tokens, P("dp", None), tokens, columns, columns, columns, split, split, lines)
        + (whole, whole, whole, columns, split, lines, whole, whole, whole),
        out_specs=(tokens, tokens, columns, columns, columns, split, split, lines, whole, whole, whole)
        + (columns, split, lines, whole, whole, whole),
        check_vma=False,
    )
```

```python
from functools import partial
import math

import jax
import jax.numpy as jnp
from jax import lax
from jax.experimental import pallas as pl
from jax.experimental.pallas import tpu as pltpu
from jax.sharding import PartitionSpec as P

HEAD_DIM = 64
LAYER_EPSILON = 1e-05
BF = jnp.bfloat16
F32 = jnp.float32


def dot(left, right, contract):
    return lax.dot_general(left, right, (contract, ((), ())), preferred_element_type=F32)


def mm(left, right):
    return dot(left, right, ((1,), (0,)))


def mm_t(left, right):
    return dot(left, right, ((1,), (1,)))


def t_mm(left, right):
    return dot(left, right, ((0,), (0,)))


def normalize(rows):
    centred = rows - jnp.mean(rows, -1, keepdims=True)
    inverse = lax.rsqrt(jnp.mean(centred * centred, -1, keepdims=True) + LAYER_EPSILON)
    return centred * inverse, inverse


def norm_backward(grad, gain, normal, inverse):
    scaled = grad * gain
    mean = jnp.mean(scaled, -1, keepdims=True)
    mean_z = jnp.mean(scaled * normal, -1, keepdims=True)
    return inverse * (scaled - mean - normal * mean_z), jnp.sum(grad * normal, 0), jnp.sum(grad, 0)


def gelu_pair(u):
    root = math.sqrt(2 / math.pi)
    t = jnp.tanh(root * (u + 0.044715 * u * u * u))
    value = 0.5 * u * (1 + t)
    slope = 0.5 * (1 + t) + 0.5 * u * (1 - t * t) * root * (1 + 3 * 0.044715 * u * u)
    return value, slope


BLOCK = 256
PAIR = 2 * HEAD_DIM


def block_dot(left, right, contract):
    return lax.dot_general(left, right, (contract, ((), ())), preferred_element_type=F32)


def forward_kernel(flags, qkv, seg_col, seg_row, context, logsum, top, total, acc, *, first, width):
    heads = width // HEAD_DIM
    blocks = qkv.shape[0] // BLOCK
    logsum[...] = jnp.zeros(logsum.shape, F32)
    for q in range(context.shape[0] // BLOCK):
        rows = slice((first + q) * BLOCK, (first + q + 1) * BLOCK)
        top[...] = jnp.full(top.shape, -1e30, F32)
        total[...] = jnp.zeros(total.shape, F32)
        acc[...] = jnp.zeros(acc.shape, F32)
        columns = seg_row[first + q]

        def step(k, carry):
            @pl.when(flags[(first + q) * blocks + k] > 0)
            def _():
                keys_at = pl.ds(pl.multiple_of(k * BLOCK, BLOCK), BLOCK)
                same = seg_col[keys_at, :] == columns
                for h in range(heads):
                    at = slice(h * HEAD_DIM, (h + 1) * HEAD_DIM)
                    query = (qkv[rows, at] * 0.125).astype(BF)
                    keys = qkv[keys_at, width + h * HEAD_DIM : width + (h + 1) * HEAD_DIM]
                    values = qkv[keys_at, 2 * width + h * HEAD_DIM : 2 * width + (h + 1) * HEAD_DIM]
                    scores = jnp.where(same, block_dot(keys, query, ((1,), (1,))), -1e30)
                    old = top[h : h + 1, :]
                    new = jnp.maximum(old, jnp.max(scores, 0, keepdims=True))
                    weights = jnp.exp(scores - new)
                    decay = jnp.exp(old - new)
                    top[h : h + 1, :] = new
                    total[h : h + 1, :] = total[h : h + 1, :] * decay + jnp.sum(weights, 0, keepdims=True)
                    acc[at, :] = acc[at, :] * decay + block_dot(values, weights.astype(BF), ((0,), (0,)))

            return carry

        lax.fori_loop(0, blocks, step, 0)
        out = slice(q * BLOCK, (q + 1) * BLOCK)
        for h in range(heads):
            at = slice(h * HEAD_DIM, (h + 1) * HEAD_DIM)
            acc[at, :] = acc[at, :] / total[h : h + 1, :]
            logsum[h : h + 1, out] = top[h : h + 1, :] + jnp.log(total[h : h + 1, :])
        context[out, :] = acc[...].T.astype(BF)


def backward_kernel(
    flags, qkv_q, qkv_k, qkv_v, seg_col, seg_row, log_a, log_b, ctx_a, ctx_b, gc_a, gc_b, grad, acc, delta, logs, gc, *, first
):
    width = qkv_q.shape[1]
    heads = width // HEAD_DIM
    blocks = qkv_q.shape[0] // BLOCK
    half = ctx_a.shape[0]
    acc[...] = jnp.zeros(acc.shape, F32)
    pick = lax.broadcasted_iota(jnp.int32, (8, width), 1) // HEAD_DIM
    pick = (pick == lax.broadcasted_iota(jnp.int32, (8, width), 0)).astype(F32)
    for index, (log, ctx, source) in enumerate(((log_a, ctx_a, gc_a), (log_b, ctx_b, gc_b))):
        gc[index * half : (index + 1) * half, :] = source[...]
        for part in range(half // BLOCK):
            at = slice(part * BLOCK, (part + 1) * BLOCK)
            product = source[at, :].astype(F32) * ctx[at, :].astype(F32)
            row = lax.dot_general(
                pick, product, (((1,), (1,)), ((), ())), precision=lax.Precision.HIGHEST, preferred_element_type=F32
            )
            delta[index * (half // BLOCK) + part] = row
            logs[index * (half // BLOCK) + part] = log[:, at]

    def step(pair, carry):
        k = pair // blocks
        q = pair % blocks

        @pl.when(flags[pair] > 0)
        def _():
            key_rows = pl.ds(pl.multiple_of(k * BLOCK, BLOCK), BLOCK)
            query_rows = pl.ds(pl.multiple_of(q * BLOCK, BLOCK), BLOCK)
            same = seg_col[key_rows, :] == seg_row[q]
            log_rows = logs[q]
            delta_rows = delta[q]
            for h in range(heads):
                at_q = slice(h * HEAD_DIM, (h + 1) * HEAD_DIM)
                at_k = slice(width + h * HEAD_DIM, width + (h + 1) * HEAD_DIM)
                at_v = slice(2 * width + h * HEAD_DIM, 2 * width + (h + 1) * HEAD_DIM)
                query = (qkv_q[query_rows, at_q] * 0.125).astype(BF)
                keys = qkv_k[key_rows, at_q]
                out = gc[query_rows, at_q]
                scores = block_dot(keys, query, ((1,), (1,)))
                weights = jnp.where(same, jnp.exp(jnp.where(same, scores, -1e30) - log_rows[first + h : first + h + 1, :]), 0.0)
                grad_weights = block_dot(qkv_v[key_rows, at_q], out, ((1,), (1,)))
                grad_scores = (weights * (grad_weights - delta_rows[h : h + 1, :])).astype(BF)
                acc[key_rows, at_v] += block_dot(weights.astype(BF), out, ((1,), (0,)))
                acc[key_rows, at_k] += block_dot(grad_scores, query, ((1,), (0,)))
                acc[query_rows, at_q] += block_dot(grad_scores, keys, ((0,), (0,)))

        return carry

    lax.fori_loop(0, blocks * blocks, step, 0)
    grad[:, :width] = (acc[:, :width] * 0.125).astype(BF)
    grad[:, width:] = acc[:, width:].astype(BF)


def attention_forward(flags, qkv, seg_col, seg_row, index, width):
    half = qkv.shape[0] // 2
    return pl.pallas_call(
        partial(forward_kernel, first=index * (half // BLOCK), width=width),
        out_shape=(jax.ShapeDtypeStruct((half, width), BF), jax.ShapeDtypeStruct((8, half), F32)),
        in_specs=[pl.BlockSpec(memory_space=pltpu.SMEM)] + [pl.BlockSpec(memory_space=pltpu.VMEM)] * 3,
        scratch_shapes=[
            pltpu.VMEM((8, BLOCK), F32),
            pltpu.VMEM((8, BLOCK), F32),
            pltpu.VMEM((width, BLOCK), F32),
        ],
        cost_estimate=pl.CostEstimate(flops=3 * 10**9, transcendentals=3 * 10**6, bytes_accessed=4 * 10**6),
        name="attention_forward",
    )(flags, qkv, seg_col, seg_row)


def attention_backward(flags, qkv, seg_col, seg_row, logs, contexts, grads, index, width):
    tokens = qkv.shape[0]
    half = tokens // 2
    count = width // PAIR
    whole = pl.BlockSpec(memory_space=pltpu.VMEM)

    def part(rows, at):
        return pl.BlockSpec((rows, PAIR), lambda i: (0, at))

    return pl.pallas_call(
        partial(backward_kernel, first=index * (PAIR // HEAD_DIM)),
        grid=(1,),
        out_shape=jax.ShapeDtypeStruct((tokens, 3 * PAIR), BF),
        in_specs=[pl.BlockSpec(memory_space=pltpu.SMEM)]
        + [part(tokens, index + count * i) for i in range(3)]
        + [whole] * 4
        + [part(half, index)] * 4,
        out_specs=pl.BlockSpec((tokens, 3 * PAIR), lambda i: (0, 0)),
        scratch_shapes=[
            pltpu.VMEM((tokens, 3 * PAIR), F32),
            pltpu.VMEM((tokens // BLOCK, 8, BLOCK), F32),
            pltpu.VMEM((tokens // BLOCK, 8, BLOCK), F32),
            pltpu.VMEM((tokens, PAIR), BF),
        ],
        cost_estimate=pl.CostEstimate(flops=5 * 10**9, transcendentals=2 * 10**6, bytes_accessed=4 * 10**6),
        name=f"attention_backward_{index}",
    )(flags, qkv, qkv, qkv, seg_col, seg_row, *logs, *contexts, *grads)


def shards(
    inputs,
    segment_ids,
    cotangent,
    w_query,
    w_key,
    w_value,
    b_query,
    b_value,
    w_out,
    b_out,
    gain_one,
    shift_one,
    w_up,
    b_up,
    w_down,
    b_down,
    gain_two,
    shift_two,
):
    ranks = lax.axis_size("tensor")
    rank = lax.axis_index("tensor")
    which = rank % 2
    rows = inputs.shape[1]
    half = 2 * rows
    width = w_query.shape[1]
    hidden_width = w_up.shape[1]
    model = inputs.shape[2]

    def inner(x):
        return lax.ppermute(x, "tensor", [(i, i ^ 1) for i in range(ranks)])

    def outer(x):
        return lax.ppermute(x, "tensor", [(i, i ^ 2) for i in range(ranks)])

    groups = lax.axis_size("dp")
    group = lax.axis_index("dp")

    def across(x, mask):
        return lax.ppermute(x, "dp", [(i, i ^ mask) for i in range(groups)])

    order = [(0, 2)] + [(i, min(4, groups >> i)) for i in range(1, groups.bit_length() - 1, 2)]

    def sum_steps(x):
        for shift, count in order:
            own = (group >> shift) % count
            part = x.shape[0] // count
            total = lax.dynamic_slice_in_dim(x, own * part, part)
            for j in range(1, count):
                send = lax.dynamic_slice_in_dim(x, (own ^ j) * part, part).astype(BF)
                total = total + across(send, j << shift).astype(F32)
            x = total
            yield x
        x = x.astype(BF)
        for shift, count in reversed(order):
            own = (group >> shift) % count
            part = x.shape[0]
            whole = jnp.zeros((part * count,) + x.shape[1:], BF)
            whole = lax.dynamic_update_slice_in_dim(whole, x, own * part, 0)
            for j in range(1, count):
                whole = lax.dynamic_update_slice_in_dim(whole, across(x, j << shift), (own ^ j) * part, 0)
            x = whole
            yield x

    def sum_groups(x):
        return list(sum_steps(x))[-1]

    def tie(x, *others):
        return lax.optimization_barrier((x,) + others)[0]

    def to_sequence(x):
        kept = jnp.where(which == 0, x[0], x[1])
        got = inner(jnp.where(which == 0, x[1], x[0]))
        return jnp.where(which == 0, jnp.concatenate([kept, got]), jnp.concatenate([got, kept]))

    def from_sequence(x):
        low, high = x[:rows], x[rows:]
        kept = jnp.where(which == 0, low, high)
        got = inner(jnp.where(which == 0, high, low))
        return jnp.where(which == 0, jnp.stack([kept, got]), jnp.stack([got, kept]))

    own_in = to_sequence(inputs)
    other_in = outer(own_in)
    own_cot = to_sequence(cotangent).astype(F32)

    def both(x, axis):
        return jnp.concatenate([x, inner(x)], axis)

    wqkv = both(jnp.concatenate([w_query, w_key, w_value], 1)[None], 0)
    wqkv = wqkv.reshape(2, model, 3, width).transpose(1, 2, 0, 3).reshape(model, 3 * 2 * width)
    bias = both(jnp.stack([b_query, b_value])[None], 0).transpose(1, 0, 2).reshape(2, 2 * width)
    bias_qkv = jnp.concatenate([bias[0], jnp.zeros((2 * width,), F32), bias[1]])
    w_out2 = both(w_out, 0)
    w_up2 = both(w_up, 1)
    b_up2 = both(b_up, 0)
    w_down2 = both(w_down, 0)

    segments = jnp.where(which == 0, segment_ids[0], segment_ids[1])
    first = jnp.where(rank // 2 == 0, segments[:half], segments[half:])
    second = jnp.where(rank // 2 == 0, segments[half:], segments[:half])
    seg = jnp.concatenate([first, second])

    blocked = seg.reshape(-1, BLOCK)
    low_id, high_id = blocked[:, 0], blocked[:, -1]
    flags = (low_id[:, None] <= high_id[None, :]) & (low_id[None, :] <= high_id[:, None])
    flags = flags.astype(jnp.int32).reshape(-1)
    seg_col = seg[:, None]
    seg_row = seg.reshape(-1, 1, BLOCK)

    def project(x):
        return (mm(x, wqkv) + bias_qkv).astype(BF)

    qkv = jnp.concatenate([project(own_in), project(other_in)])
    context_other, log_other = attention_forward(flags, qkv, seg_col, seg_row, 1, 2 * width)
    got = outer(mm(context_other, w_out2).astype(BF))
    context_own, log_own = attention_forward(flags, qkv, seg_col, seg_row, 0, 2 * width)
    attended = mm(context_own, w_out2) + got.astype(F32) + b_out
    normal_one, inverse_one = normalize(own_in.astype(F32) + attended)
    hidden_one = normal_one * gain_one + shift_one
    low_own = hidden_one.astype(BF)
    low_other = outer(low_own)

    def feed(low):
        value, slope = gelu_pair(mm(low, w_up2) + b_up2)
        return value.astype(BF), slope

    act_own, slope_own = feed(low_own)
    act_other, slope_other = feed(low_other)
    got = outer(mm(act_other, w_down2).astype(BF))
    branch = mm(act_own, w_down2) + got.astype(F32) + b_down
    normal_two, inverse_two = normalize(hidden_one + branch)
    output = (normal_two * gain_two + shift_two).astype(BF)

    grad_two, grad_gain_two, grad_shift_two = norm_backward(own_cot, gain_two, normal_two, inverse_two)
    gb_own = grad_two.astype(BF)
    grad_b_down = jnp.sum(gb_own.astype(F32), 0)
    gb_other = outer(gb_own)
    before_own = (mm_t(gb_own, w_down2) * slope_own).astype(BF)
    before_other = (mm_t(gb_other, w_down2) * slope_other).astype(BF)
    got = outer(mm_t(before_other, w_up2).astype(BF))
    grad_w_down = t_mm(act_own, gb_own) + t_mm(act_other, gb_other)
    grad_w_up = t_mm(low_own, before_own) + t_mm(low_other, before_other)
    grad_b_up = jnp.sum(before_own.astype(F32), 0) + jnp.sum(before_other.astype(F32), 0)
    grad_hidden = mm_t(before_own, w_up2) + got.astype(F32) + grad_two
    grad_one, grad_gain_one, grad_shift_one = norm_backward(grad_hidden, gain_one, normal_one, inverse_one)
    ga_own = grad_one.astype(BF)
    grad_b_out = jnp.sum(ga_own.astype(F32), 0)
    ga_other = outer(ga_own)

    def pair_sum(mine, theirs):
        return mine + inner(theirs.astype(BF)).astype(F32)

    down = list(sum_steps(pair_sum(grad_w_down[:hidden_width], grad_w_down[hidden_width:])))
    up = list(sum_steps(pair_sum(grad_w_up[:, :hidden_width], grad_w_up[:, hidden_width:])))
    ga_other = tie(ga_other, down[0], up[0])
    grad_w_out = t_mm(context_own, ga_own) + t_mm(context_other, ga_other)

    gc_own = mm_t(ga_own, w_out2).astype(BF)
    gc_other = mm_t(ga_other, w_out2).astype(BF)
    pairs = []
    for index in range(2 * width // PAIR):
        ready = tie(flags, down[min(index, len(down) - 1)], up[min(index, len(up) - 1)])
        pairs.append(
            attention_backward(
                ready,
                qkv,
                seg_col,
                seg_row,
                (log_own, log_other),
                (context_own, context_other),
                (gc_own, gc_other),
                index,
                2 * width,
            )
        )
    gqkv = jnp.concatenate([x[:, i * PAIR : (i + 1) * PAIR] for i in range(3) for x in pairs], 1)
    gqkv_own, gqkv_other = gqkv[:half], gqkv[half:]
    got = outer(mm_t(gqkv_other, wqkv).astype(BF))
    grad_wqkv = t_mm(gqkv_own, own_in) + t_mm(gqkv_other, other_in)
    grad_bqkv = jnp.sum(gqkv_own.astype(F32), 0) + jnp.sum(gqkv_other.astype(F32), 0)
    grad_input = mm_t(gqkv_own, wqkv) + got.astype(F32) + grad_one

    by_part = grad_wqkv.reshape(3, 2, width, model)
    mine = jnp.concatenate([by_part[0, 0], by_part[1, 0], by_part[2, 0], grad_w_out[:width]])
    theirs = jnp.concatenate([by_part[0, 1], by_part[1, 1], by_part[2, 1], grad_w_out[width:]])
    grad_attention = pair_sum(mine, theirs)
    cut = 2 * width
    grad_qkv = jnp.concatenate([sum_groups(grad_attention[:cut]), sum_groups(grad_attention[cut:])])
    grad_qkv = grad_qkv.astype(F32)

    shared = jnp.stack(
        [grad_b_out, grad_gain_one, grad_shift_one, grad_b_down, grad_gain_two, grad_shift_two]
    )
    shared = lax.optimization_barrier((shared, gqkv_other))[0]
    shared = shared + inner(shared)
    shared = shared + outer(shared)
    bias_parts = grad_bqkv.reshape(3, 2, width)
    mine = jnp.concatenate([bias_parts[0, 0], bias_parts[2, 0], grad_b_up[:hidden_width]])
    theirs = jnp.concatenate([bias_parts[0, 1], bias_parts[2, 1], grad_b_up[hidden_width:]])
    small = jnp.concatenate([shared.reshape(-1), mine + inner(theirs)])
    for bit in range(groups.bit_length() - 1):
        small = small + across(small, 1 << bit)
    shared = small[: 6 * model].reshape(6, model)
    small = small[6 * model :]

    return (
        from_sequence(output),
        from_sequence(grad_input),
        grad_qkv[:width].T,
        grad_qkv[width : 2 * width].T,
        grad_qkv[2 * width : 3 * width].T,
        small[:width],
        small[width : 2 * width],
        grad_qkv[3 * width :],
        shared[0],
        shared[1],
        shared[2],
        up[-1].astype(F32),
        small[2 * width :],
        down[-1].astype(F32),
        shared[3],
        shared[4],
        shared[5],
    )


def solution(mesh):
    tokens = P("dp", "tensor", None)
    columns = P(None, "tensor")
    lines = P("tensor", None)
    split = P("tensor")
    whole = P()
    return jax.shard_map(
        shards,
        mesh=mesh,
        in_specs=(tokens, P("dp", None), tokens, columns, columns, columns, split, split, lines)
        + (whole, whole, whole, columns, split, lines, whole, whole, whole),
        out_specs=(tokens, tokens, columns, columns, columns, split, split, lines, whole, whole, whole)
        + (columns, split, lines, whole, whole, whole),
        check_vma=False,
    )
```

```python
from functools import partial
import math

import jax
import jax.numpy as jnp
from jax import lax
from jax.experimental import pallas as pl
from jax.experimental.pallas import tpu as pltpu
from jax.sharding import PartitionSpec as P

HEAD_DIM = 64
LAYER_EPSILON = 1e-05
BF = jnp.bfloat16
F32 = jnp.float32


def dot(left, right, contract):
    return lax.dot_general(left, right, (contract, ((), ())), preferred_element_type=F32)


def mm(left, right):
    return dot(left, right, ((1,), (0,)))


def mm_t(left, right):
    return dot(left, right, ((1,), (1,)))


def t_mm(left, right):
    return dot(left, right, ((0,), (0,)))


def normalize(rows):
    centred = rows - jnp.mean(rows, -1, keepdims=True)
    inverse = lax.rsqrt(jnp.mean(centred * centred, -1, keepdims=True) + LAYER_EPSILON)
    return centred * inverse, inverse


def norm_backward(grad, gain, normal, inverse):
    scaled = grad * gain
    mean = jnp.mean(scaled, -1, keepdims=True)
    mean_z = jnp.mean(scaled * normal, -1, keepdims=True)
    return inverse * (scaled - mean - normal * mean_z), jnp.sum(grad * normal, 0), jnp.sum(grad, 0)


def gelu_pair(u):
    root = math.sqrt(2 / math.pi)
    t = jnp.tanh(root * (u + 0.044715 * u * u * u))
    value = 0.5 * u * (1 + t)
    slope = 0.5 * (1 + t) + 0.5 * u * (1 - t * t) * root * (1 + 3 * 0.044715 * u * u)
    return value, slope


BLOCK = 256


def block_dot(left, right, contract):
    return lax.dot_general(left, right, (contract, ((), ())), preferred_element_type=F32)


def forward_kernel(flags, qkv, seg_col, seg_row, context, logsum, top, total, acc, *, first, width):
    heads = width // HEAD_DIM
    blocks = qkv.shape[0] // BLOCK
    logsum[...] = jnp.zeros(logsum.shape, F32)
    for q in range(context.shape[0] // BLOCK):
        rows = slice((first + q) * BLOCK, (first + q + 1) * BLOCK)
        top[...] = jnp.full(top.shape, -1e30, F32)
        total[...] = jnp.zeros(total.shape, F32)
        acc[...] = jnp.zeros(acc.shape, F32)
        columns = seg_row[first + q]

        def step(k, carry):
            @pl.when(flags[(first + q) * blocks + k] > 0)
            def _():
                keys_at = pl.ds(pl.multiple_of(k * BLOCK, BLOCK), BLOCK)
                same = seg_col[keys_at, :] == columns
                for h in range(heads):
                    at = slice(h * HEAD_DIM, (h + 1) * HEAD_DIM)
                    query = (qkv[rows, at] * 0.125).astype(BF)
                    keys = qkv[keys_at, width + h * HEAD_DIM : width + (h + 1) * HEAD_DIM]
                    values = qkv[keys_at, 2 * width + h * HEAD_DIM : 2 * width + (h + 1) * HEAD_DIM]
                    scores = jnp.where(same, block_dot(keys, query, ((1,), (1,))), -1e30)
                    old = top[h : h + 1, :]
                    new = jnp.maximum(old, jnp.max(scores, 0, keepdims=True))
                    weights = jnp.exp(scores - new)
                    decay = jnp.exp(old - new)
                    top[h : h + 1, :] = new
                    total[h : h + 1, :] = total[h : h + 1, :] * decay + jnp.sum(weights, 0, keepdims=True)
                    acc[at, :] = acc[at, :] * decay + block_dot(values, weights.astype(BF), ((0,), (0,)))

            return carry

        lax.fori_loop(0, blocks, step, 0)
        out = slice(q * BLOCK, (q + 1) * BLOCK)
        for h in range(heads):
            at = slice(h * HEAD_DIM, (h + 1) * HEAD_DIM)
            acc[at, :] = acc[at, :] / total[h : h + 1, :]
            logsum[h : h + 1, out] = top[h : h + 1, :] + jnp.log(total[h : h + 1, :])
        context[out, :] = acc[...].T.astype(BF)


def backward_kernel(
    flags, qkv_q, qkv_k, qkv_v, seg_col, seg_row, log_a, log_b, ctx_a, ctx_b, gc_a, gc_b, grad, acc, delta, logs, gc, *, first
):
    width = qkv_q.shape[1]
    heads = width // HEAD_DIM
    blocks = qkv_q.shape[0] // BLOCK
    half = ctx_a.shape[0]
    acc[...] = jnp.zeros(acc.shape, F32)
    pick = lax.broadcasted_iota(jnp.int32, (8, width), 1) // HEAD_DIM
    pick = (pick == lax.broadcasted_iota(jnp.int32, (8, width), 0)).astype(F32)
    for index, (log, ctx, source) in enumerate(((log_a, ctx_a, gc_a), (log_b, ctx_b, gc_b))):
        gc[index * half : (index + 1) * half, :] = source[...]
        for part in range(half // BLOCK):
            at = slice(part * BLOCK, (part + 1) * BLOCK)
            product = source[at, :].astype(F32) * ctx[at, :].astype(F32)
            row = lax.dot_general(
                pick, product, (((1,), (1,)), ((), ())), precision=lax.Precision.HIGHEST, preferred_element_type=F32
            )
            delta[index * (half // BLOCK) + part] = row
            logs[index * (half // BLOCK) + part] = log[:, at]

    def step(pair, carry):
        k = pair // blocks
        q = pair % blocks

        @pl.when(flags[pair] > 0)
        def _():
            key_rows = pl.ds(pl.multiple_of(k * BLOCK, BLOCK), BLOCK)
            query_rows = pl.ds(pl.multiple_of(q * BLOCK, BLOCK), BLOCK)
            same = seg_col[key_rows, :] == seg_row[q]
            log_rows = logs[q]
            delta_rows = delta[q]
            for h in range(heads):
                at_q = slice(h * HEAD_DIM, (h + 1) * HEAD_DIM)
                at_k = slice(width + h * HEAD_DIM, width + (h + 1) * HEAD_DIM)
                at_v = slice(2 * width + h * HEAD_DIM, 2 * width + (h + 1) * HEAD_DIM)
                query = (qkv_q[query_rows, at_q] * 0.125).astype(BF)
                keys = qkv_k[key_rows, at_q]
                out = gc[query_rows, at_q]
                scores = block_dot(keys, query, ((1,), (1,)))
                weights = jnp.where(same, jnp.exp(jnp.where(same, scores, -1e30) - log_rows[first + h : first + h + 1, :]), 0.0)
                grad_weights = block_dot(qkv_v[key_rows, at_q], out, ((1,), (1,)))
                grad_scores = (weights * (grad_weights - delta_rows[h : h + 1, :])).astype(BF)
                acc[key_rows, at_v] += block_dot(weights.astype(BF), out, ((1,), (0,)))
                acc[key_rows, at_k] += block_dot(grad_scores, query, ((1,), (0,)))
                acc[query_rows, at_q] += block_dot(grad_scores, keys, ((0,), (0,)))

        return carry

    lax.fori_loop(0, blocks * blocks, step, 0)
    grad[:, :width] = (acc[:, :width] * 0.125).astype(BF)
    grad[:, width:] = acc[:, width:].astype(BF)


def attention_forward(flags, qkv, seg_col, seg_row, index, width):
    half = qkv.shape[0] // 2
    return pl.pallas_call(
        partial(forward_kernel, first=index * (half // BLOCK), width=width),
        out_shape=(jax.ShapeDtypeStruct((half, width), BF), jax.ShapeDtypeStruct((8, half), F32)),
        in_specs=[pl.BlockSpec(memory_space=pltpu.SMEM)] + [pl.BlockSpec(memory_space=pltpu.VMEM)] * 3,
        scratch_shapes=[
            pltpu.VMEM((8, BLOCK), F32),
            pltpu.VMEM((8, BLOCK), F32),
            pltpu.VMEM((width, BLOCK), F32),
        ],
        cost_estimate=pl.CostEstimate(flops=3 * 10**9, transcendentals=3 * 10**6, bytes_accessed=4 * 10**6),
        name="attention_forward",
    )(flags, qkv, seg_col, seg_row)


def attention_backward(flags, qkv, seg_col, seg_row, logs, contexts, grads, width):
    tokens = qkv.shape[0]
    half = tokens // 2
    index, count = 0, 1
    whole = pl.BlockSpec(memory_space=pltpu.VMEM)

    def part(rows, at):
        return pl.BlockSpec((rows, width), lambda i: (0, at))

    return pl.pallas_call(
        partial(backward_kernel, first=index * (width // HEAD_DIM)),
        grid=(1,),
        out_shape=jax.ShapeDtypeStruct((tokens, 3 * width), BF),
        in_specs=[pl.BlockSpec(memory_space=pltpu.SMEM)]
        + [part(tokens, index + count * i) for i in range(3)]
        + [whole] * 4
        + [part(half, index)] * 4,
        out_specs=pl.BlockSpec((tokens, 3 * width), lambda i: (0, 0)),
        scratch_shapes=[
            pltpu.VMEM((tokens, 3 * width), F32),
            pltpu.VMEM((tokens // BLOCK, 8, BLOCK), F32),
            pltpu.VMEM((tokens // BLOCK, 8, BLOCK), F32),
            pltpu.VMEM((tokens, width), BF),
        ],
        cost_estimate=pl.CostEstimate(flops=15 * 10**9, transcendentals=6 * 10**6, bytes_accessed=4 * 10**6),
        name="attention_backward",
    )(flags, qkv, qkv, qkv, seg_col, seg_row, *logs, *contexts, *grads)


def shards(
    inputs,
    segment_ids,
    cotangent,
    w_query,
    w_key,
    w_value,
    b_query,
    b_value,
    w_out,
    b_out,
    gain_one,
    shift_one,
    w_up,
    b_up,
    w_down,
    b_down,
    gain_two,
    shift_two,
):
    ranks = lax.axis_size("tensor")
    rank = lax.axis_index("tensor")
    which = rank % 2
    rows = inputs.shape[1]
    half = 2 * rows
    width = w_query.shape[1]
    hidden_width = w_up.shape[1]
    model = inputs.shape[2]

    def inner(x):
        return lax.ppermute(x, "tensor", [(i, i ^ 1) for i in range(ranks)])

    def outer(x):
        return lax.ppermute(x, "tensor", [(i, i ^ 2) for i in range(ranks)])

    groups = lax.axis_size("dp")
    group = lax.axis_index("dp")

    def across(x, mask):
        return lax.ppermute(x, "dp", [(i, i ^ mask) for i in range(groups)])

    def sum_groups(x, order):
        for shift, count in order:
            own = (group >> shift) % count
            part = x.shape[0] // count
            total = lax.dynamic_slice_in_dim(x, own * part, part)
            for j in range(1, count):
                send = lax.dynamic_slice_in_dim(x, (own ^ j) * part, part).astype(BF)
                total = total + across(send, j << shift).astype(F32)
            x = total
        x = x.astype(BF)
        for shift, count in reversed(order):
            own = (group >> shift) % count
            part = x.shape[0]
            whole = jnp.zeros((part * count,) + x.shape[1:], BF)
            whole = lax.dynamic_update_slice_in_dim(whole, x, own * part, 0)
            for j in range(1, count):
                whole = lax.dynamic_update_slice_in_dim(whole, across(x, j << shift), (own ^ j) * part, 0)
            x = whole
        return x

    def to_sequence(x):
        kept = jnp.where(which == 0, x[0], x[1])
        got = inner(jnp.where(which == 0, x[1], x[0]))
        return jnp.where(which == 0, jnp.concatenate([kept, got]), jnp.concatenate([got, kept]))

    def from_sequence(x):
        low, high = x[:rows], x[rows:]
        kept = jnp.where(which == 0, low, high)
        got = inner(jnp.where(which == 0, high, low))
        return jnp.where(which == 0, jnp.stack([kept, got]), jnp.stack([got, kept]))

    own_in = to_sequence(inputs)
    other_in = outer(own_in)
    own_cot = to_sequence(cotangent).astype(F32)

    def both(x, axis):
        return jnp.concatenate([x, inner(x)], axis)

    wqkv = both(jnp.concatenate([w_query, w_key, w_value], 1)[None], 0)
    wqkv = wqkv.reshape(2, model, 3, width).transpose(1, 2, 0, 3).reshape(model, 3 * 2 * width)
    bias = both(jnp.stack([b_query, b_value])[None], 0).transpose(1, 0, 2).reshape(2, 2 * width)
    bias_qkv = jnp.concatenate([bias[0], jnp.zeros((2 * width,), F32), bias[1]])
    w_out2 = both(w_out, 0)
    w_up2 = both(w_up, 1)
    b_up2 = both(b_up, 0)
    w_down2 = both(w_down, 0)

    segments = jnp.where(which == 0, segment_ids[0], segment_ids[1])
    first = jnp.where(rank // 2 == 0, segments[:half], segments[half:])
    second = jnp.where(rank // 2 == 0, segments[half:], segments[:half])
    seg = jnp.concatenate([first, second])

    blocked = seg.reshape(-1, BLOCK)
    low_id, high_id = blocked[:, 0], blocked[:, -1]
    flags = (low_id[:, None] <= high_id[None, :]) & (low_id[None, :] <= high_id[:, None])
    flags = flags.astype(jnp.int32).reshape(-1)
    seg_col = seg[:, None]
    seg_row = seg.reshape(-1, 1, BLOCK)

    def project(x):
        return (mm(x, wqkv) + bias_qkv).astype(BF)

    qkv = jnp.concatenate([project(own_in), project(other_in)])
    context_other, log_other = attention_forward(flags, qkv, seg_col, seg_row, 1, 2 * width)
    got = outer(mm(context_other, w_out2).astype(BF))
    context_own, log_own = attention_forward(flags, qkv, seg_col, seg_row, 0, 2 * width)
    attended = mm(context_own, w_out2) + got.astype(F32) + b_out
    normal_one, inverse_one = normalize(own_in.astype(F32) + attended)
    hidden_one = normal_one * gain_one + shift_one
    low_own = hidden_one.astype(BF)
    low_other = outer(low_own)

    def feed(low):
        value, slope = gelu_pair(mm(low, w_up2) + b_up2)
        return value.astype(BF), slope

    act_own, slope_own = feed(low_own)
    act_other, slope_other = feed(low_other)
    got = outer(mm(act_other, w_down2).astype(BF))
    branch = mm(act_own, w_down2) + got.astype(F32) + b_down
    normal_two, inverse_two = normalize(hidden_one + branch)
    output = (normal_two * gain_two + shift_two).astype(BF)

    grad_two, grad_gain_two, grad_shift_two = norm_backward(own_cot, gain_two, normal_two, inverse_two)
    gb_own = grad_two.astype(BF)
    grad_b_down = jnp.sum(gb_own.astype(F32), 0)
    gb_other = outer(gb_own)
    before_own = (mm_t(gb_own, w_down2) * slope_own).astype(BF)
    before_other = (mm_t(gb_other, w_down2) * slope_other).astype(BF)
    got = outer(mm_t(before_other, w_up2).astype(BF))
    grad_w_down = t_mm(act_own, gb_own) + t_mm(act_other, gb_other)
    grad_w_up = t_mm(low_own, before_own) + t_mm(low_other, before_other)
    grad_b_up = jnp.sum(before_own.astype(F32), 0) + jnp.sum(before_other.astype(F32), 0)
    grad_hidden = mm_t(before_own, w_up2) + got.astype(F32) + grad_two
    grad_one, grad_gain_one, grad_shift_one = norm_backward(grad_hidden, gain_one, normal_one, inverse_one)
    ga_own = grad_one.astype(BF)
    grad_b_out = jnp.sum(ga_own.astype(F32), 0)
    ga_other = outer(ga_own)

    def pair_sum(mine, theirs):
        return mine + inner(theirs.astype(BF)).astype(F32)

    grad_w_up = pair_sum(grad_w_up[:, :hidden_width], grad_w_up[:, hidden_width:])
    grad_w_down = pair_sum(grad_w_down[:hidden_width], grad_w_down[hidden_width:])
    summed = (grad_w_up.astype(BF), grad_w_down.astype(BF))
    ga_own_late, summed = lax.optimization_barrier((ga_own, summed))
    grad_w_up, grad_w_down = lax.psum(summed, "dp")
    grad_w_out = t_mm(context_own, ga_own_late) + t_mm(context_other, ga_other)
    order = [(0, 2)] + [(i, min(4, groups >> i)) for i in range(1, groups.bit_length() - 1, 2)]
    orders = (order, order[::-1])

    gc_own = mm_t(ga_own, w_out2).astype(BF)
    gc_other = mm_t(ga_other, w_out2).astype(BF)
    gqkv = attention_backward(
        flags, qkv, seg_col, seg_row, (log_own, log_other), (context_own, context_other), (gc_own, gc_other), 2 * width
    )
    gqkv_own, gqkv_other = gqkv[:half], gqkv[half:]
    got = outer(mm_t(gqkv_other, wqkv).astype(BF))
    grad_wqkv = t_mm(gqkv_own, own_in) + t_mm(gqkv_other, other_in)
    grad_bqkv = jnp.sum(gqkv_own.astype(F32), 0) + jnp.sum(gqkv_other.astype(F32), 0)
    grad_input = mm_t(gqkv_own, wqkv) + got.astype(F32) + grad_one

    by_part = grad_wqkv.reshape(3, 2, width, model)
    mine = jnp.concatenate([by_part[0, 0], by_part[1, 0], by_part[2, 0], grad_w_out[:width]])
    theirs = jnp.concatenate([by_part[0, 1], by_part[1, 1], by_part[2, 1], grad_w_out[width:]])
    grad_qkv = pair_sum(mine, theirs)
    cut = 2 * width
    grad_qkv = jnp.concatenate([sum_groups(grad_qkv[:cut], orders[0]), sum_groups(grad_qkv[cut:], orders[1])])
    grad_qkv = grad_qkv.astype(F32)

    shared = jnp.stack(
        [grad_b_out, grad_gain_one, grad_shift_one, grad_b_down, grad_gain_two, grad_shift_two]
    )
    shared = lax.optimization_barrier((shared, gqkv_other))[0]
    shared = shared + inner(shared)
    shared = shared + outer(shared)
    bias_parts = grad_bqkv.reshape(3, 2, width)
    mine = jnp.concatenate([bias_parts[0, 0], bias_parts[2, 0], grad_b_up[:hidden_width]])
    theirs = jnp.concatenate([bias_parts[0, 1], bias_parts[2, 1], grad_b_up[hidden_width:]])
    small = jnp.concatenate([shared.reshape(-1), mine + inner(theirs)])
    for bit in range(groups.bit_length() - 1):
        small = small + across(small, 1 << bit)
    shared = small[: 6 * model].reshape(6, model)
    small = small[6 * model :]

    return (
        from_sequence(output),
        from_sequence(grad_input),
        grad_qkv[:width].T,
        grad_qkv[width : 2 * width].T,
        grad_qkv[2 * width : 3 * width].T,
        small[:width],
        small[width : 2 * width],
        grad_qkv[3 * width :],
        shared[0],
        shared[1],
        shared[2],
        grad_w_up.astype(F32),
        small[2 * width :],
        grad_w_down.astype(F32),
        shared[3],
        shared[4],
        shared[5],
    )


def solution(mesh):
    tokens = P("dp", "tensor", None)
    columns = P(None, "tensor")
    lines = P("tensor", None)
    split = P("tensor")
    whole = P()
    return jax.shard_map(
        shards,
        mesh=mesh,
        in_specs=(tokens, P("dp", None), tokens, columns, columns, columns, split, split, lines)
        + (whole, whole, whole, columns, split, lines, whole, whole, whole),
        out_specs=(tokens, tokens, columns, columns, columns, split, split, lines, whole, whole, whole)
        + (columns, split, lines, whole, whole, whole),
        check_vma=False,
    )
```

```python
from functools import partial
import math

import jax
import jax.numpy as jnp
from jax import lax
from jax.experimental import pallas as pl
from jax.experimental.pallas import tpu as pltpu
from jax.sharding import PartitionSpec as P

HEAD_DIM = 64
LAYER_EPSILON = 1e-05
BF = jnp.bfloat16
F32 = jnp.float32


def dot(left, right, contract):
    return lax.dot_general(left, right, (contract, ((), ())), preferred_element_type=F32)


def mm(left, right):
    return dot(left, right, ((1,), (0,)))


def mm_t(left, right):
    return dot(left, right, ((1,), (1,)))


def t_mm(left, right):
    return dot(left, right, ((0,), (0,)))


def normalize(rows):
    centred = rows - jnp.mean(rows, -1, keepdims=True)
    inverse = lax.rsqrt(jnp.mean(centred * centred, -1, keepdims=True) + LAYER_EPSILON)
    return centred * inverse, inverse


def norm_backward(grad, gain, normal, inverse):
    scaled = grad * gain
    mean = jnp.mean(scaled, -1, keepdims=True)
    mean_z = jnp.mean(scaled * normal, -1, keepdims=True)
    return inverse * (scaled - mean - normal * mean_z), jnp.sum(grad * normal, 0), jnp.sum(grad, 0)


def gelu_pair(u):
    root = math.sqrt(2 / math.pi)
    t = jnp.tanh(root * (u + 0.044715 * u * u * u))
    value = 0.5 * u * (1 + t)
    slope = 0.5 * (1 + t) + 0.5 * u * (1 - t * t) * root * (1 + 3 * 0.044715 * u * u)
    return value, slope


BLOCK = 256


def block_dot(left, right, contract):
    return lax.dot_general(left, right, (contract, ((), ())), preferred_element_type=F32)


def forward_kernel(flags, qkv, seg_col, seg_row, *refs, skip, first, span, keys_from, keys_to, resumed, final, width):
    heads = width // HEAD_DIM
    refs = refs[skip:]
    before = refs[:3] if resumed else None
    out = refs[3:] if resumed else refs
    top, total, acc = out[-3:]
    for q in range(acc.shape[0]):
        rows = slice((first + q) * BLOCK, (first + q + 1) * BLOCK)
        if resumed:
            top[q] = before[0][q]
            total[q] = before[1][q]
            acc[q] = before[2][q]
        else:
            top[q] = jnp.full(top.shape[1:], -1e30, F32)
            total[q] = jnp.zeros(total.shape[1:], F32)
            acc[q] = jnp.zeros(acc.shape[1:], F32)
        columns = seg_row[first + q]

        def step(k, carry):
            @pl.when(flags[(first + q) * span + k] > 0)
            def _():
                keys_at = pl.ds(pl.multiple_of(k * BLOCK, BLOCK), BLOCK)
                same = seg_col[keys_at, :] == columns
                for h in range(heads):
                    at = slice(h * HEAD_DIM, (h + 1) * HEAD_DIM)
                    row = slice(h, h + 1)
                    query = (qkv[rows, at] * 0.125).astype(BF)
                    keys = qkv[keys_at, width + h * HEAD_DIM : width + (h + 1) * HEAD_DIM]
                    values = qkv[keys_at, 2 * width + h * HEAD_DIM : 2 * width + (h + 1) * HEAD_DIM]
                    scores = jnp.where(same, block_dot(keys, query, ((1,), (1,))), -1e30)
                    old = top[q, row, :]
                    new = jnp.maximum(old, jnp.max(scores, 0, keepdims=True))
                    weights = jnp.exp(scores - new)
                    decay = jnp.exp(old - new)
                    top[q, row, :] = new
                    total[q, row, :] = total[q, row, :] * decay + jnp.sum(weights, 0, keepdims=True)
                    acc[q, at, :] = acc[q, at, :] * decay + block_dot(values, weights.astype(BF), ((0,), (0,)))

            return carry

        lax.fori_loop(keys_from, keys_to, step, 0)
        if final:
            context, logsum = out[:2]
            place = slice(q * BLOCK, (q + 1) * BLOCK)
            logsum[:, place] = jnp.zeros((8, BLOCK), F32)
            for h in range(heads):
                at = slice(h * HEAD_DIM, (h + 1) * HEAD_DIM)
                row = slice(h, h + 1)
                acc[q, at, :] = acc[q, at, :] / total[q, row, :]
                logsum[row, place] = top[q, row, :] + jnp.log(total[q, row, :])
            context[place, :] = acc[q].T.astype(BF)


def attention_forward(flags, qkv, seg_col, seg_row, width, name, first, keys, state=None, final=True, after=()):
    half = seg_col.shape[0] // 2
    count = half // BLOCK
    shapes = [(count, 8, BLOCK), (count, 8, BLOCK), (count, width, BLOCK)]
    if final:
        out_shape = (jax.ShapeDtypeStruct((half, width), BF), jax.ShapeDtypeStruct((8, half), F32))
        scratch = [pltpu.VMEM(shape, F32) for shape in shapes]
    else:
        out_shape = tuple(jax.ShapeDtypeStruct(shape, F32) for shape in shapes)
        scratch = []
    state = () if state is None else state
    weight = keys[1] - keys[0]
    return pl.pallas_call(
        partial(
            forward_kernel,
            skip=len(after),
            first=first * count,
            span=2 * count,
            keys_from=keys[0] * count,
            keys_to=keys[1] * count,
            resumed=len(state) > 0,
            final=final,
            width=width,
        ),
        out_shape=out_shape,
        in_specs=[pl.BlockSpec(memory_space=pltpu.SMEM)] + [pl.BlockSpec(memory_space=pltpu.VMEM)] * 3
        + [pl.BlockSpec(memory_space=pl.ANY)] * len(after)
        + [pl.BlockSpec(memory_space=pltpu.VMEM)] * len(state),
        scratch_shapes=scratch,
        cost_estimate=pl.CostEstimate(
            flops=weight * 3 * 10**9, transcendentals=weight * 2 * 10**6, bytes_accessed=4 * 10**6
        ),
        name=name,
    )(flags, qkv, seg_col, seg_row, *after, *state)


def backward_kernel(flags, qkv, seg_col, seg_row, log, ctx, gc, *refs, first, resumed, width):
    heads = width // HEAD_DIM
    tokens, half = qkv.shape[0], ctx.shape[0]
    blocks, count = tokens // BLOCK, half // BLOCK
    if resumed:
        before_q, before_kv, grad, acc_q, acc_kv, delta = refs
        acc_kv[...] = before_kv[...]
    else:
        out_q, acc_kv, acc_q, delta = refs
        acc_kv[...] = jnp.zeros(acc_kv.shape, F32)
    acc_q[...] = jnp.zeros(acc_q.shape, F32)
    pick = lax.broadcasted_iota(jnp.int32, (8, width), 1) // HEAD_DIM
    pick = (pick == lax.broadcasted_iota(jnp.int32, (8, width), 0)).astype(F32)
    for part in range(count):
        at = slice(part * BLOCK, (part + 1) * BLOCK)
        product = gc[at, :].astype(F32) * ctx[at, :].astype(F32)
        delta[0, part] = lax.dot_general(
            pick, product, (((1,), (1,)), ((), ())), precision=lax.Precision.HIGHEST, preferred_element_type=F32
        )
        delta[1, part] = log[:, at]

    def step(pair, carry):
        k = pair // count
        q = pair % count

        @pl.when(flags[k * blocks + first + q] > 0)
        def _():
            key_rows = pl.ds(pl.multiple_of(k * BLOCK, BLOCK), BLOCK)
            query_rows = pl.ds(pl.multiple_of((first + q) * BLOCK, BLOCK), BLOCK)
            own_rows = pl.ds(pl.multiple_of(q * BLOCK, BLOCK), BLOCK)
            same = seg_col[key_rows, :] == seg_row[first + q]
            delta_rows = delta[0, q]
            log_rows = delta[1, q]
            for h in range(heads):
                at_q = slice(h * HEAD_DIM, (h + 1) * HEAD_DIM)
                at_k = slice(width + h * HEAD_DIM, width + (h + 1) * HEAD_DIM)
                at_v = slice(2 * width + h * HEAD_DIM, 2 * width + (h + 1) * HEAD_DIM)
                query = (qkv[query_rows, at_q] * 0.125).astype(BF)
                keys = qkv[key_rows, at_k]
                out = gc[own_rows, at_q]
                scores = block_dot(keys, query, ((1,), (1,)))
                weights = jnp.where(same, jnp.exp(jnp.where(same, scores, -1e30) - log_rows[h : h + 1, :]), 0.0)
                grad_weights = block_dot(qkv[key_rows, at_v], out, ((1,), (1,)))
                grad_scores = (weights * (grad_weights - delta_rows[h : h + 1, :])).astype(BF)
                acc_kv[key_rows, at_k] += block_dot(weights.astype(BF), out, ((1,), (0,)))
                acc_kv[key_rows, at_q] += block_dot(grad_scores, query, ((1,), (0,)))
                acc_q[own_rows, at_q] += block_dot(grad_scores, keys, ((0,), (0,)))

        return carry

    lax.fori_loop(0, blocks * count, step, 0)
    grad_q = (acc_q[...] * 0.125).astype(BF)
    if resumed:
        grad[:half, :width] = before_q[...]
        grad[half:, :width] = grad_q
        grad[:, width:] = acc_kv[...].astype(BF)
    else:
        out_q[...] = grad_q


def attention_backward(flags, qkv, seg_col, seg_row, log, context, grad, width, before=()):
    tokens = qkv.shape[0]
    half = tokens // 2
    resumed = len(before) > 0
    scratch = [pltpu.VMEM((half, width), F32), pltpu.VMEM((2, half // BLOCK, 8, BLOCK), F32)]
    if resumed:
        out_shape = jax.ShapeDtypeStruct((tokens, 3 * width), BF)
        scratch.insert(1, pltpu.VMEM((tokens, 2 * width), F32))
    else:
        out_shape = (jax.ShapeDtypeStruct((half, width), BF), jax.ShapeDtypeStruct((tokens, 2 * width), F32))
    return pl.pallas_call(
        partial(backward_kernel, first=half // BLOCK if resumed else 0, resumed=resumed, width=width),
        out_shape=out_shape,
        in_specs=[pl.BlockSpec(memory_space=pltpu.SMEM)] + [pl.BlockSpec(memory_space=pltpu.VMEM)] * (6 + len(before)),
        scratch_shapes=scratch,
        cost_estimate=pl.CostEstimate(flops=8 * 10**9, transcendentals=3 * 10**6, bytes_accessed=8 * 10**6),
        name="attention_backward_other" if resumed else "attention_backward_own",
    )(flags, qkv, seg_col, seg_row, log, context, grad, *before)


def shards(
    inputs,
    segment_ids,
    cotangent,
    w_query,
    w_key,
    w_value,
    b_query,
    b_value,
    w_out,
    b_out,
    gain_one,
    shift_one,
    w_up,
    b_up,
    w_down,
    b_down,
    gain_two,
    shift_two,
):
    ranks = lax.axis_size("tensor")
    rank = lax.axis_index("tensor")
    which = rank % 2
    rows = inputs.shape[1]
    half = 2 * rows
    width = w_query.shape[1]
    hidden_width = w_up.shape[1]
    model = inputs.shape[2]

    def inner(x):
        return lax.ppermute(x, "tensor", [(i, i ^ 1) for i in range(ranks)])

    def outer(x):
        return lax.ppermute(x, "tensor", [(i, i ^ 2) for i in range(ranks)])

    groups = lax.axis_size("dp")
    group = lax.axis_index("dp")

    def across(x, mask):
        return lax.ppermute(x, "dp", [(i, i ^ mask) for i in range(groups)])

    def sum_groups(x, order):
        for shift, count in order:
            own = (group >> shift) % count
            part = x.shape[0] // count
            total = lax.dynamic_slice_in_dim(x, own * part, part)
            for j in range(1, count):
                send = lax.dynamic_slice_in_dim(x, (own ^ j) * part, part).astype(BF)
                total = total + across(send, j << shift).astype(F32)
            x = total
        x = x.astype(BF)
        for shift, count in reversed(order):
            own = (group >> shift) % count
            part = x.shape[0]
            whole = jnp.zeros((part * count,) + x.shape[1:], BF)
            whole = lax.dynamic_update_slice_in_dim(whole, x, own * part, 0)
            for j in range(1, count):
                whole = lax.dynamic_update_slice_in_dim(whole, across(x, j << shift), (own ^ j) * part, 0)
            x = whole
        return x

    def to_sequence(x):
        kept = jnp.where(which == 0, x[0], x[1])
        got = inner(jnp.where(which == 0, x[1], x[0]))
        return jnp.where(which == 0, jnp.concatenate([kept, got]), jnp.concatenate([got, kept]))

    def from_sequence(x):
        low, high = x[:rows], x[rows:]
        kept = jnp.where(which == 0, low, high)
        got = inner(jnp.where(which == 0, high, low))
        return jnp.where(which == 0, jnp.stack([kept, got]), jnp.stack([got, kept]))

    own_in = to_sequence(inputs)
    straight = outer(jnp.where(which == 0, inputs[0], inputs[1]))
    crossed = jnp.where(which == 0, inputs[1], inputs[0])
    crossed = lax.ppermute(crossed, "tensor", [(i, i ^ 3) for i in range(ranks)])
    other_in = jnp.where(
        which == 0, jnp.concatenate([straight, crossed]), jnp.concatenate([crossed, straight])
    )
    own_cot = to_sequence(cotangent).astype(F32)

    def both(x, axis):
        return jnp.concatenate([x, inner(x)], axis)

    wqkv = both(jnp.concatenate([w_query, w_key, w_value], 1)[None], 0)
    wqkv = wqkv.reshape(2, model, 3, width).transpose(1, 2, 0, 3).reshape(model, 3 * 2 * width)
    bias = both(jnp.stack([b_query, b_value])[None], 0).transpose(1, 0, 2).reshape(2, 2 * width)
    bias_qkv = jnp.concatenate([bias[0], jnp.zeros((2 * width,), F32), bias[1]])
    w_out2 = both(w_out, 0)
    w_up2 = both(w_up, 1)
    b_up2 = both(b_up, 0)
    w_down2 = both(w_down, 0)

    segments = jnp.where(which == 0, segment_ids[0], segment_ids[1])
    first = jnp.where(rank // 2 == 0, segments[:half], segments[half:])
    second = jnp.where(rank // 2 == 0, segments[half:], segments[:half])
    seg = jnp.concatenate([first, second])

    blocked = seg.reshape(-1, BLOCK)
    low_id, high_id = blocked[:, 0], blocked[:, -1]
    flags = (low_id[:, None] <= high_id[None, :]) & (low_id[None, :] <= high_id[:, None])
    flags = flags.astype(jnp.int32).reshape(-1)
    seg_col = seg[:, None]
    seg_row = seg.reshape(-1, 1, BLOCK)

    def project(x):
        return (mm(x, wqkv) + bias_qkv).astype(BF)

    qkv_own = project(own_in)
    state = attention_forward(
        flags, qkv_own, seg_col, seg_row, 2 * width, "attention_own_own", 0, (0, 1), final=False
    )
    qkv = jnp.concatenate([qkv_own, project(other_in)])
    context_other, log_other = attention_forward(
        flags, qkv, seg_col, seg_row, 2 * width, "attention_other_all", 1, (0, 2), after=state[:1]
    )
    got = outer(mm(context_other, w_out2).astype(BF))
    context_own, log_own = attention_forward(
        flags, qkv, seg_col, seg_row, 2 * width, "attention_own_other", 0, (1, 2), state=state
    )
    attended = mm(context_own, w_out2) + got.astype(F32) + b_out
    normal_one, inverse_one = normalize(own_in.astype(F32) + attended)
    hidden_one = normal_one * gain_one + shift_one
    low_own = hidden_one.astype(BF)
    low_other = outer(low_own)

    def feed(low):
        value, slope = gelu_pair(mm(low, w_up2) + b_up2)
        return value.astype(BF), slope

    act_own, slope_own = feed(low_own)
    act_other, slope_other = feed(low_other)
    got = outer(mm(act_other, w_down2).astype(BF))
    branch = mm(act_own, w_down2) + got.astype(F32) + b_down
    normal_two, inverse_two = normalize(hidden_one + branch)
    output = (normal_two * gain_two + shift_two).astype(BF)

    grad_two, grad_gain_two, grad_shift_two = norm_backward(own_cot, gain_two, normal_two, inverse_two)
    gb_own = grad_two.astype(BF)
    grad_b_down = jnp.sum(gb_own.astype(F32), 0)
    gb_other = outer(gb_own)
    before_own = (mm_t(gb_own, w_down2) * slope_own).astype(BF)
    before_other = (mm_t(gb_other, w_down2) * slope_other).astype(BF)
    got = outer(mm_t(before_other, w_up2).astype(BF))
    grad_w_down = t_mm(act_own, gb_own) + t_mm(act_other, gb_other)
    grad_w_up = t_mm(low_own, before_own) + t_mm(low_other, before_other)
    grad_b_up = jnp.sum(before_own.astype(F32), 0) + jnp.sum(before_other.astype(F32), 0)
    grad_hidden = mm_t(before_own, w_up2) + got.astype(F32) + grad_two
    grad_one, grad_gain_one, grad_shift_one = norm_backward(grad_hidden, gain_one, normal_one, inverse_one)
    ga_own = grad_one.astype(BF)
    grad_b_out = jnp.sum(ga_own.astype(F32), 0)
    ga_other = outer(ga_own)

    def pair_sum(mine, theirs):
        return mine + inner(theirs.astype(BF)).astype(F32)

    grad_w_up = pair_sum(grad_w_up[:, :hidden_width], grad_w_up[:, hidden_width:])
    grad_w_down = pair_sum(grad_w_down[:hidden_width], grad_w_down[hidden_width:])
    summed = (grad_w_up.astype(BF), grad_w_down.astype(BF))
    ga_own_late, summed = lax.optimization_barrier((ga_own, summed))
    grad_w_up, grad_w_down = lax.psum(summed, "dp")
    grad_w_out = t_mm(context_own, ga_own_late) + t_mm(context_other, ga_other)
    order = [(0, 2)] + [(i, min(4, groups >> i)) for i in range(1, groups.bit_length() - 1, 2)]
    orders = (order, order[::-1])

    gc_own = mm_t(ga_own, w_out2).astype(BF)
    gc_other = mm_t(ga_other, w_out2).astype(BF)
    before = attention_backward(flags, qkv, seg_col, seg_row, log_own, context_own, gc_own, 2 * width)
    gqkv = attention_backward(
        flags, qkv, seg_col, seg_row, log_other, context_other, gc_other, 2 * width, before=before
    )
    gqkv_own, gqkv_other = gqkv[:half], gqkv[half:]
    got = outer(mm_t(gqkv_other, wqkv).astype(BF))
    grad_wqkv = t_mm(gqkv_own, own_in) + t_mm(gqkv_other, other_in)
    grad_bqkv = jnp.sum(gqkv_own.astype(F32), 0) + jnp.sum(gqkv_other.astype(F32), 0)
    grad_input = mm_t(gqkv_own, wqkv) + got.astype(F32) + grad_one

    by_part = grad_wqkv.reshape(3, 2, width, model)
    mine = jnp.concatenate([by_part[0, 0], by_part[1, 0], by_part[2, 0], grad_w_out[:width]])
    theirs = jnp.concatenate([by_part[0, 1], by_part[1, 1], by_part[2, 1], grad_w_out[width:]])
    grad_qkv = pair_sum(mine, theirs)
    cut = 2 * width
    grad_qkv = jnp.concatenate([sum_groups(grad_qkv[:cut], orders[0]), sum_groups(grad_qkv[cut:], orders[1])])
    grad_qkv = grad_qkv.astype(F32)

    shared = jnp.stack(
        [grad_b_out, grad_gain_one, grad_shift_one, grad_b_down, grad_gain_two, grad_shift_two]
    )
    shared = lax.optimization_barrier((shared, gqkv_other))[0]
    shared = shared + inner(shared)
    shared = shared + outer(shared)
    bias_parts = grad_bqkv.reshape(3, 2, width)
    mine = jnp.concatenate([bias_parts[0, 0], bias_parts[2, 0], grad_b_up[:hidden_width]])
    theirs = jnp.concatenate([bias_parts[0, 1], bias_parts[2, 1], grad_b_up[hidden_width:]])
    small = jnp.concatenate([shared.reshape(-1), mine + inner(theirs)])
    for bit in range(groups.bit_length() - 1):
        small = small + across(small, 1 << bit)
    shared = small[: 6 * model].reshape(6, model)
    small = small[6 * model :]

    return (
        from_sequence(output),
        from_sequence(grad_input),
        grad_qkv[:width].T,
        grad_qkv[width : 2 * width].T,
        grad_qkv[2 * width : 3 * width].T,
        small[:width],
        small[width : 2 * width],
        grad_qkv[3 * width :],
        shared[0],
        shared[1],
        shared[2],
        grad_w_up.astype(F32),
        small[2 * width :],
        grad_w_down.astype(F32),
        shared[3],
        shared[4],
        shared[5],
    )


def solution(mesh):
    tokens = P("dp", "tensor", None)
    columns = P(None, "tensor")
    lines = P("tensor", None)
    split = P("tensor")
    whole = P()
    return jax.shard_map(
        shards,
        mesh=mesh,
        in_specs=(tokens, P("dp", None), tokens, columns, columns, columns, split, split, lines)
        + (whole, whole, whole, columns, split, lines, whole, whole, whole),
        out_specs=(tokens, tokens, columns, columns, columns, split, split, lines, whole, whole, whole)
        + (columns, split, lines, whole, whole, whole),
        check_vma=False,
    )
```

```python
from functools import partial
import math

import jax
import jax.numpy as jnp
from jax import lax
from jax.experimental import pallas as pl
from jax.experimental.pallas import tpu as pltpu
from jax.sharding import PartitionSpec as P

HEAD_DIM = 64
LAYER_EPSILON = 1e-05
BF = jnp.bfloat16
F32 = jnp.float32


def dot(left, right, contract):
    return lax.dot_general(left, right, (contract, ((), ())), preferred_element_type=F32)


def mm(left, right):
    return dot(left, right, ((1,), (0,)))


def mm_t(left, right):
    return dot(left, right, ((1,), (1,)))


def t_mm(left, right):
    return dot(left, right, ((0,), (0,)))


def normalize(rows):
    centred = rows - jnp.mean(rows, -1, keepdims=True)
    inverse = lax.rsqrt(jnp.mean(centred * centred, -1, keepdims=True) + LAYER_EPSILON)
    return centred * inverse, inverse


def norm_backward(grad, gain, normal, inverse):
    scaled = grad * gain
    mean = jnp.mean(scaled, -1, keepdims=True)
    mean_z = jnp.mean(scaled * normal, -1, keepdims=True)
    return inverse * (scaled - mean - normal * mean_z), jnp.sum(grad * normal, 0), jnp.sum(grad, 0)


def gelu_pair(u):
    root = math.sqrt(2 / math.pi)
    t = jnp.tanh(root * (u + 0.044715 * u * u * u))
    value = 0.5 * u * (1 + t)
    slope = 0.5 * (1 + t) + 0.5 * u * (1 - t * t) * root * (1 + 3 * 0.044715 * u * u)
    return value, slope


BLOCK = 256


def block_dot(left, right, contract):
    return lax.dot_general(left, right, (contract, ((), ())), preferred_element_type=F32)


def forward_kernel(flags, qkv, seg_col, seg_row, *refs, skip, first, span, keys_from, keys_to, resumed, final, width):
    heads = width // HEAD_DIM
    refs = refs[skip:]
    before = refs[:3] if resumed else None
    out = refs[3:] if resumed else refs
    top, total, acc = out[-3:]
    for q in range(acc.shape[0]):
        rows = slice((first + q) * BLOCK, (first + q + 1) * BLOCK)
        if resumed:
            top[q] = before[0][q]
            total[q] = before[1][q]
            acc[q] = before[2][q]
        else:
            top[q] = jnp.full(top.shape[1:], -1e30, F32)
            total[q] = jnp.zeros(total.shape[1:], F32)
            acc[q] = jnp.zeros(acc.shape[1:], F32)
        columns = seg_row[first + q]

        def step(k, carry):
            @pl.when(flags[(first + q) * span + k] > 0)
            def _():
                keys_at = pl.ds(pl.multiple_of(k * BLOCK, BLOCK), BLOCK)
                same = seg_col[keys_at, :] == columns
                for h in range(heads):
                    at = slice(h * HEAD_DIM, (h + 1) * HEAD_DIM)
                    row = slice(h, h + 1)
                    query = (qkv[rows, at] * 0.125).astype(BF)
                    keys = qkv[keys_at, width + h * HEAD_DIM : width + (h + 1) * HEAD_DIM]
                    values = qkv[keys_at, 2 * width + h * HEAD_DIM : 2 * width + (h + 1) * HEAD_DIM]
                    scores = jnp.where(same, block_dot(keys, query, ((1,), (1,))), -1e30)
                    old = top[q, row, :]
                    new = jnp.maximum(old, jnp.max(scores, 0, keepdims=True))
                    weights = jnp.exp(scores - new)
                    decay = jnp.exp(old - new)
                    top[q, row, :] = new
                    total[q, row, :] = total[q, row, :] * decay + jnp.sum(weights, 0, keepdims=True)
                    acc[q, at, :] = acc[q, at, :] * decay + block_dot(values, weights.astype(BF), ((0,), (0,)))

            return carry

        lax.fori_loop(keys_from, keys_to, step, 0)
        if final:
            context, logsum = out[:2]
            place = slice(q * BLOCK, (q + 1) * BLOCK)
            logsum[:, place] = jnp.zeros((8, BLOCK), F32)
            for h in range(heads):
                at = slice(h * HEAD_DIM, (h + 1) * HEAD_DIM)
                row = slice(h, h + 1)
                acc[q, at, :] = acc[q, at, :] / total[q, row, :]
                logsum[row, place] = top[q, row, :] + jnp.log(total[q, row, :])
            context[place, :] = acc[q].T.astype(BF)


def attention_forward(flags, qkv, seg_col, seg_row, width, name, first, keys, state=None, final=True, after=()):
    half = seg_col.shape[0] // 2
    count = half // BLOCK
    shapes = [(count, 8, BLOCK), (count, 8, BLOCK), (count, width, BLOCK)]
    if final:
        out_shape = (jax.ShapeDtypeStruct((half, width), BF), jax.ShapeDtypeStruct((8, half), F32))
        scratch = [pltpu.VMEM(shape, F32) for shape in shapes]
    else:
        out_shape = tuple(jax.ShapeDtypeStruct(shape, F32) for shape in shapes)
        scratch = []
    state = () if state is None else state
    weight = keys[1] - keys[0]
    return pl.pallas_call(
        partial(
            forward_kernel,
            skip=len(after),
            first=first * count,
            span=2 * count,
            keys_from=keys[0] * count,
            keys_to=keys[1] * count,
            resumed=len(state) > 0,
            final=final,
            width=width,
        ),
        out_shape=out_shape,
        in_specs=[pl.BlockSpec(memory_space=pltpu.SMEM)] + [pl.BlockSpec(memory_space=pltpu.VMEM)] * 3
        + [pl.BlockSpec(memory_space=pl.ANY)] * len(after)
        + [pl.BlockSpec(memory_space=pltpu.VMEM)] * len(state),
        scratch_shapes=scratch,
        cost_estimate=pl.CostEstimate(
            flops=weight * 3 * 10**9, transcendentals=weight * 2 * 10**6, bytes_accessed=4 * 10**6
        ),
        name=name,
    )(flags, qkv, seg_col, seg_row, *after, *state)


def backward_kernel(flags, qkv, seg_col, seg_row, log, ctx, gc, *refs, first, resumed, width):
    heads = width // HEAD_DIM
    tokens, half = qkv.shape[0], ctx.shape[0]
    blocks, count = tokens // BLOCK, half // BLOCK
    if resumed:
        before_q, before_kv, grad, acc_q, acc_kv, delta = refs
        acc_kv[...] = before_kv[...]
    else:
        out_q, acc_kv, acc_q, delta = refs
        acc_kv[...] = jnp.zeros(acc_kv.shape, F32)
    acc_q[...] = jnp.zeros(acc_q.shape, F32)
    pick = lax.broadcasted_iota(jnp.int32, (8, width), 1) // HEAD_DIM
    pick = (pick == lax.broadcasted_iota(jnp.int32, (8, width), 0)).astype(F32)
    for part in range(count):
        at = slice(part * BLOCK, (part + 1) * BLOCK)
        product = gc[at, :].astype(F32) * ctx[at, :].astype(F32)
        delta[0, part] = lax.dot_general(
            pick, product, (((1,), (1,)), ((), ())), precision=lax.Precision.HIGHEST, preferred_element_type=F32
        )
        delta[1, part] = log[:, at]

    def step(pair, carry):
        k = pair // count
        q = pair % count

        @pl.when(flags[k * blocks + first + q] > 0)
        def _():
            key_rows = pl.ds(pl.multiple_of(k * BLOCK, BLOCK), BLOCK)
            query_rows = pl.ds(pl.multiple_of((first + q) * BLOCK, BLOCK), BLOCK)
            own_rows = pl.ds(pl.multiple_of(q * BLOCK, BLOCK), BLOCK)
            same = seg_col[key_rows, :] == seg_row[first + q]
            delta_rows = delta[0, q]
            log_rows = delta[1, q]
            for h in range(heads):
                at_q = slice(h * HEAD_DIM, (h + 1) * HEAD_DIM)
                at_k = slice(width + h * HEAD_DIM, width + (h + 1) * HEAD_DIM)
                at_v = slice(2 * width + h * HEAD_DIM, 2 * width + (h + 1) * HEAD_DIM)
                query = (qkv[query_rows, at_q] * 0.125).astype(BF)
                keys = qkv[key_rows, at_k]
                out = gc[own_rows, at_q]
                scores = block_dot(keys, query, ((1,), (1,)))
                weights = jnp.where(same, jnp.exp(jnp.where(same, scores, -1e30) - log_rows[h : h + 1, :]), 0.0)
                grad_weights = block_dot(qkv[key_rows, at_v], out, ((1,), (1,)))
                grad_scores = (weights * (grad_weights - delta_rows[h : h + 1, :])).astype(BF)
                acc_kv[key_rows, at_k] += block_dot(weights.astype(BF), out, ((1,), (0,)))
                acc_kv[key_rows, at_q] += block_dot(grad_scores, query, ((1,), (0,)))
                acc_q[own_rows, at_q] += block_dot(grad_scores, keys, ((0,), (0,)))

        return carry

    lax.fori_loop(0, blocks * count, step, 0)
    grad_q = (acc_q[...] * 0.125).astype(BF)
    if resumed:
        grad[:half, :width] = before_q[...]
        grad[half:, :width] = grad_q
        grad[:, width:] = acc_kv[...].astype(BF)
    else:
        out_q[...] = grad_q


def attention_backward(flags, qkv, seg_col, seg_row, log, context, grad, width, before=()):
    tokens = qkv.shape[0]
    half = tokens // 2
    resumed = len(before) > 0
    scratch = [pltpu.VMEM((half, width), F32), pltpu.VMEM((2, half // BLOCK, 8, BLOCK), F32)]
    if resumed:
        out_shape = jax.ShapeDtypeStruct((tokens, 3 * width), BF)
        scratch.insert(1, pltpu.VMEM((tokens, 2 * width), F32))
    else:
        out_shape = (jax.ShapeDtypeStruct((half, width), BF), jax.ShapeDtypeStruct((tokens, 2 * width), F32))
    return pl.pallas_call(
        partial(backward_kernel, first=half // BLOCK if resumed else 0, resumed=resumed, width=width),
        out_shape=out_shape,
        in_specs=[pl.BlockSpec(memory_space=pltpu.SMEM)] + [pl.BlockSpec(memory_space=pltpu.VMEM)] * (6 + len(before)),
        scratch_shapes=scratch,
        cost_estimate=pl.CostEstimate(flops=8 * 10**9, transcendentals=3 * 10**6, bytes_accessed=8 * 10**6),
        name="attention_backward_other" if resumed else "attention_backward_own",
    )(flags, qkv, seg_col, seg_row, log, context, grad, *before)


def shards(
    inputs,
    segment_ids,
    cotangent,
    w_query,
    w_key,
    w_value,
    b_query,
    b_value,
    w_out,
    b_out,
    gain_one,
    shift_one,
    w_up,
    b_up,
    w_down,
    b_down,
    gain_two,
    shift_two,
):
    ranks = lax.axis_size("tensor")
    rank = lax.axis_index("tensor")
    which = rank % 2
    rows = inputs.shape[1]
    half = 2 * rows
    width = w_query.shape[1]
    hidden_width = w_up.shape[1]
    model = inputs.shape[2]

    def inner(x):
        return lax.ppermute(x, "tensor", [(i, i ^ 1) for i in range(ranks)])

    def outer(x):
        return lax.ppermute(x, "tensor", [(i, i ^ 2) for i in range(ranks)])

    groups = lax.axis_size("dp")
    group = lax.axis_index("dp")

    def across(x, mask):
        return lax.ppermute(x, "dp", [(i, i ^ mask) for i in range(groups)])

    def sum_groups(x, order):
        started = []
        for shift, count in order:
            own = (group >> shift) % count
            part = x.shape[0] // count
            total = lax.dynamic_slice_in_dim(x, own * part, part)
            for j in range(1, count):
                send = lax.dynamic_slice_in_dim(x, (own ^ j) * part, part).astype(BF)
                total = total + across(send, j << shift).astype(F32)
            x = total
            started.append(x[0, 0])
        x = x.astype(BF)
        for shift, count in reversed(order):
            own = (group >> shift) % count
            part = x.shape[0]
            whole = jnp.zeros((part * count,) + x.shape[1:], BF)
            whole = lax.dynamic_update_slice_in_dim(whole, x, own * part, 0)
            for j in range(1, count):
                whole = lax.dynamic_update_slice_in_dim(whole, across(x, j << shift), (own ^ j) * part, 0)
            x = whole
        return x, started

    def to_sequence(x):
        kept = jnp.where(which == 0, x[0], x[1])
        got = inner(jnp.where(which == 0, x[1], x[0]))
        return jnp.where(which == 0, jnp.concatenate([kept, got]), jnp.concatenate([got, kept]))

    def from_sequence(x):
        low, high = x[:rows], x[rows:]
        kept = jnp.where(which == 0, low, high)
        got = inner(jnp.where(which == 0, high, low))
        return jnp.where(which == 0, jnp.stack([kept, got]), jnp.stack([got, kept]))

    own_in = to_sequence(inputs)
    straight = outer(jnp.where(which == 0, inputs[0], inputs[1]))
    crossed = jnp.where(which == 0, inputs[1], inputs[0])
    crossed = lax.ppermute(crossed, "tensor", [(i, i ^ 3) for i in range(ranks)])
    other_in = jnp.where(
        which == 0, jnp.concatenate([straight, crossed]), jnp.concatenate([crossed, straight])
    )
    own_cot = to_sequence(cotangent).astype(F32)

    def both(x, axis):
        return jnp.concatenate([x, inner(x)], axis)

    wqkv = both(jnp.concatenate([w_query, w_key, w_value], 1)[None], 0)
    wqkv = wqkv.reshape(2, model, 3, width).transpose(1, 2, 0, 3).reshape(model, 3 * 2 * width)
    bias = both(jnp.stack([b_query, b_value])[None], 0).transpose(1, 0, 2).reshape(2, 2 * width)
    bias_qkv = jnp.concatenate([bias[0], jnp.zeros((2 * width,), F32), bias[1]])
    w_out2 = both(w_out, 0)
    w_up2 = both(w_up, 1)
    b_up2 = both(b_up, 0)
    w_down2 = both(w_down, 0)

    segments = jnp.where(which == 0, segment_ids[0], segment_ids[1])
    first = jnp.where(rank // 2 == 0, segments[:half], segments[half:])
    second = jnp.where(rank // 2 == 0, segments[half:], segments[:half])
    seg = jnp.concatenate([first, second])

    blocked = seg.reshape(-1, BLOCK)
    low_id, high_id = blocked[:, 0], blocked[:, -1]
    flags = (low_id[:, None] <= high_id[None, :]) & (low_id[None, :] <= high_id[:, None])
    flags = flags.astype(jnp.int32).reshape(-1)
    seg_col = seg[:, None]
    seg_row = seg.reshape(-1, 1, BLOCK)

    def project(x):
        return (mm(x, wqkv) + bias_qkv).astype(BF)

    qkv_own = project(own_in)
    state = attention_forward(
        flags, qkv_own, seg_col, seg_row, 2 * width, "attention_own_own", 0, (0, 1), final=False
    )
    qkv = jnp.concatenate([qkv_own, project(other_in)])
    context_other, log_other = attention_forward(
        flags, qkv, seg_col, seg_row, 2 * width, "attention_other_all", 1, (0, 2), after=state[:1]
    )
    got = outer(mm(context_other, w_out2).astype(BF))
    context_own, log_own = attention_forward(
        flags, qkv, seg_col, seg_row, 2 * width, "attention_own_other", 0, (1, 2), state=state
    )
    attended = mm(context_own, w_out2) + got.astype(F32) + b_out
    normal_one, inverse_one = normalize(own_in.astype(F32) + attended)
    hidden_one = normal_one * gain_one + shift_one
    low_own = hidden_one.astype(BF)
    low_other = outer(low_own)

    def feed(low):
        value, slope = gelu_pair(mm(low, w_up2) + b_up2)
        return value.astype(BF), slope

    act_own, slope_own = feed(low_own)
    act_other, slope_other = feed(low_other)
    got = outer(mm(act_other, w_down2).astype(BF))
    branch = mm(act_own, w_down2) + got.astype(F32) + b_down
    normal_two, inverse_two = normalize(hidden_one + branch)
    output = (normal_two * gain_two + shift_two).astype(BF)

    grad_two, grad_gain_two, grad_shift_two = norm_backward(own_cot, gain_two, normal_two, inverse_two)
    gb_own = grad_two.astype(BF)
    grad_b_down = jnp.sum(gb_own.astype(F32), 0)
    gb_other = outer(gb_own)
    before_own = (mm_t(gb_own, w_down2) * slope_own).astype(BF)
    before_other = (mm_t(gb_other, w_down2) * slope_other).astype(BF)
    got = outer(mm_t(before_other, w_up2).astype(BF))
    grad_w_down = t_mm(act_own, gb_own) + t_mm(act_other, gb_other)
    grad_w_up = t_mm(low_own, before_own) + t_mm(low_other, before_other)
    grad_b_up = jnp.sum(before_own.astype(F32), 0) + jnp.sum(before_other.astype(F32), 0)

    def pair_sum(mine, theirs):
        return mine + inner(theirs.astype(BF)).astype(F32)

    def zero_after(x):
        return jnp.where(x != x, 1.0, 0.0).astype(F32)

    grad_w_up = pair_sum(grad_w_up[:, :hidden_width], grad_w_up[:, hidden_width:]).astype(BF)
    grad_w_down = pair_sum(grad_w_down[:hidden_width], grad_w_down[hidden_width:]).astype(BF)
    late = zero_after(grad_w_up[0, 0]) + zero_after(grad_w_down[0, 0])
    grad_w_up, grad_w_down = lax.psum((grad_w_up, grad_w_down), "dp")
    grad_hidden = mm_t(before_own, w_up2) + got.astype(F32) + (grad_two + late)
    grad_one, grad_gain_one, grad_shift_one = norm_backward(grad_hidden, gain_one, normal_one, inverse_one)
    ga_own = grad_one.astype(BF)
    grad_b_out = jnp.sum(ga_own.astype(F32), 0)
    ga_other = outer(ga_own)

    grad_w_out = t_mm(context_own, ga_own) + t_mm(context_other, ga_other)
    order = [(0, 2)] + [(i, min(4, groups >> i)) for i in range(1, groups.bit_length() - 1, 2)]

    gc_own = mm_t(ga_own, w_out2).astype(BF)
    gc_other = mm_t(ga_other, w_out2).astype(BF)
    before = attention_backward(flags, qkv, seg_col, seg_row, log_own, context_own, gc_own, 2 * width)
    gqkv = attention_backward(
        flags, qkv, seg_col, seg_row, log_other, context_other, gc_other, 2 * width, before=before
    )
    gqkv_own, gqkv_other = gqkv[:half], gqkv[half:]
    got = outer(mm_t(gqkv_other, wqkv).astype(BF))
    grad_wqkv = t_mm(gqkv_own, own_in) + t_mm(gqkv_other, other_in)
    grad_bqkv = jnp.sum(gqkv_own.astype(F32), 0) + jnp.sum(gqkv_other.astype(F32), 0)

    by_part = grad_wqkv.reshape(3, 2, width, model)
    mine = jnp.concatenate([by_part[0, 0], by_part[1, 0], by_part[2, 0], grad_w_out[:width]])
    theirs = jnp.concatenate([by_part[0, 1], by_part[1, 1], by_part[2, 1], grad_w_out[width:]])
    grad_qkv, started = sum_groups(pair_sum(mine, theirs), order)
    grad_qkv = grad_qkv.astype(F32)

    shared = jnp.stack(
        [grad_b_out, grad_gain_one, grad_shift_one, grad_b_down, grad_gain_two, grad_shift_two]
    )
    shared = shared + zero_after(started[0])
    grad_input = mm_t(gqkv_own, wqkv) + got.astype(F32) + (grad_one + zero_after(started[1]))
    shared = shared + inner(shared)
    shared = shared + outer(shared)
    bias_parts = grad_bqkv.reshape(3, 2, width)
    mine = jnp.concatenate([bias_parts[0, 0], bias_parts[2, 0], grad_b_up[:hidden_width]])
    theirs = jnp.concatenate([bias_parts[0, 1], bias_parts[2, 1], grad_b_up[hidden_width:]])
    small = jnp.concatenate([shared.reshape(-1), mine + inner(theirs)])
    for bit in range(groups.bit_length() - 1):
        small = small + across(small, 1 << bit)
    shared = small[: 6 * model].reshape(6, model)
    small = small[6 * model :]

    return (
        from_sequence(output),
        from_sequence(grad_input),
        grad_qkv[:width].T,
        grad_qkv[width : 2 * width].T,
        grad_qkv[2 * width : 3 * width].T,
        small[:width],
        small[width : 2 * width],
        grad_qkv[3 * width :],
        shared[0],
        shared[1],
        shared[2],
        grad_w_up.astype(F32),
        small[2 * width :],
        grad_w_down.astype(F32),
        shared[3],
        shared[4],
        shared[5],
    )


def solution(mesh):
    tokens = P("dp", "tensor", None)
    columns = P(None, "tensor")
    lines = P("tensor", None)
    split = P("tensor")
    whole = P()
    return jax.shard_map(
        shards,
        mesh=mesh,
        in_specs=(tokens, P("dp", None), tokens, columns, columns, columns, split, split, lines)
        + (whole, whole, whole, columns, split, lines, whole, whole, whole),
        out_specs=(tokens, tokens, columns, columns, columns, split, split, lines, whole, whole, whole)
        + (columns, split, lines, whole, whole, whole),
        check_vma=False,
    )
```

```python
from functools import partial
import math

import jax
import jax.numpy as jnp
from jax import lax
from jax.experimental import pallas as pl
from jax.experimental.pallas import tpu as pltpu
from jax.sharding import PartitionSpec as P

HEAD_DIM = 64
LAYER_EPSILON = 1e-05
BF = jnp.bfloat16
F32 = jnp.float32


def dot(left, right, contract):
    return lax.dot_general(left, right, (contract, ((), ())), preferred_element_type=F32)


def mm(left, right):
    return dot(left, right, ((1,), (0,)))


def mm_t(left, right):
    return dot(left, right, ((1,), (1,)))


def t_mm(left, right):
    return dot(left, right, ((0,), (0,)))


def normalize(rows):
    centred = rows - jnp.mean(rows, -1, keepdims=True)
    inverse = lax.rsqrt(jnp.mean(centred * centred, -1, keepdims=True) + LAYER_EPSILON)
    return centred * inverse, inverse


def norm_backward(grad, gain, normal, inverse):
    scaled = grad * gain
    mean = jnp.mean(scaled, -1, keepdims=True)
    mean_z = jnp.mean(scaled * normal, -1, keepdims=True)
    return inverse * (scaled - mean - normal * mean_z), jnp.sum(grad * normal, 0), jnp.sum(grad, 0)


def gelu_pair(u):
    root = math.sqrt(2 / math.pi)
    t = jnp.tanh(root * (u + 0.044715 * u * u * u))
    value = 0.5 * u * (1 + t)
    slope = 0.5 * (1 + t) + 0.5 * u * (1 - t * t) * root * (1 + 3 * 0.044715 * u * u)
    return value, slope


BLOCK = 256


def block_dot(left, right, contract):
    return lax.dot_general(left, right, (contract, ((), ())), preferred_element_type=F32)


def forward_kernel(flags, qkv, seg_col, seg_row, *refs, skip, first, span, keys_from, keys_to, resumed, final, width):
    heads = width // HEAD_DIM
    refs = refs[skip:]
    before = refs[:3] if resumed else None
    out = refs[3:] if resumed else refs
    top, total, acc = out[-3:]
    for q in range(acc.shape[0]):
        rows = slice((first + q) * BLOCK, (first + q + 1) * BLOCK)
        if resumed:
            top[q] = before[0][q]
            total[q] = before[1][q]
            acc[q] = before[2][q]
        else:
            top[q] = jnp.full(top.shape[1:], -1e30, F32)
            total[q] = jnp.zeros(total.shape[1:], F32)
            acc[q] = jnp.zeros(acc.shape[1:], F32)
        columns = seg_row[first + q]

        def step(k, carry):
            @pl.when(flags[(first + q) * span + k] > 0)
            def _():
                keys_at = pl.ds(pl.multiple_of(k * BLOCK, BLOCK), BLOCK)
                same = seg_col[keys_at, :] == columns
                for h in range(heads):
                    at = slice(h * HEAD_DIM, (h + 1) * HEAD_DIM)
                    row = slice(h, h + 1)
                    query = (qkv[rows, at] * 0.125).astype(BF)
                    keys = qkv[keys_at, width + h * HEAD_DIM : width + (h + 1) * HEAD_DIM]
                    values = qkv[keys_at, 2 * width + h * HEAD_DIM : 2 * width + (h + 1) * HEAD_DIM]
                    scores = jnp.where(same, block_dot(keys, query, ((1,), (1,))), -1e30)
                    old = top[q, row, :]
                    new = jnp.maximum(old, jnp.max(scores, 0, keepdims=True))
                    weights = jnp.exp(scores - new)
                    decay = jnp.exp(old - new)
                    top[q, row, :] = new
                    total[q, row, :] = total[q, row, :] * decay + jnp.sum(weights, 0, keepdims=True)
                    acc[q, at, :] = acc[q, at, :] * decay + block_dot(values, weights.astype(BF), ((0,), (0,)))

            return carry

        lax.fori_loop(keys_from, keys_to, step, 0)
        if final:
            context, logsum = out[:2]
            place = slice(q * BLOCK, (q + 1) * BLOCK)
            logsum[:, place] = jnp.zeros((8, BLOCK), F32)
            for h in range(heads):
                at = slice(h * HEAD_DIM, (h + 1) * HEAD_DIM)
                row = slice(h, h + 1)
                acc[q, at, :] = acc[q, at, :] / total[q, row, :]
                logsum[row, place] = top[q, row, :] + jnp.log(total[q, row, :])
            context[place, :] = acc[q].T.astype(BF)


def attention_forward(flags, qkv, seg_col, seg_row, width, name, first, keys, state=None, final=True, after=()):
    half = seg_col.shape[0] // 2
    count = half // BLOCK
    shapes = [(count, 8, BLOCK), (count, 8, BLOCK), (count, width, BLOCK)]
    if final:
        out_shape = (jax.ShapeDtypeStruct((half, width), BF), jax.ShapeDtypeStruct((8, half), F32))
        scratch = [pltpu.VMEM(shape, F32) for shape in shapes]
    else:
        out_shape = tuple(jax.ShapeDtypeStruct(shape, F32) for shape in shapes)
        scratch = []
    state = () if state is None else state
    weight = keys[1] - keys[0]
    return pl.pallas_call(
        partial(
            forward_kernel,
            skip=len(after),
            first=first * count,
            span=2 * count,
            keys_from=keys[0] * count,
            keys_to=keys[1] * count,
            resumed=len(state) > 0,
            final=final,
            width=width,
        ),
        out_shape=out_shape,
        in_specs=[pl.BlockSpec(memory_space=pltpu.SMEM)] + [pl.BlockSpec(memory_space=pltpu.VMEM)] * 3
        + [pl.BlockSpec(memory_space=pl.ANY)] * len(after)
        + [pl.BlockSpec(memory_space=pltpu.VMEM)] * len(state),
        scratch_shapes=scratch,
        cost_estimate=pl.CostEstimate(
            flops=weight * 3 * 10**9, transcendentals=weight * 2 * 10**6, bytes_accessed=4 * 10**6
        ),
        name=name,
    )(flags, qkv, seg_col, seg_row, *after, *state)


def backward_kernel(flags, qkv, seg_col, seg_row, log, ctx, gc, *refs, first, resumed, width):
    heads = width // HEAD_DIM
    tokens, half = qkv.shape[0], ctx.shape[0]
    blocks, count = tokens // BLOCK, half // BLOCK
    if resumed:
        before_q, before_kv, grad, acc_q, acc_kv, delta = refs
        acc_kv[...] = before_kv[...]
    else:
        out_q, acc_kv, acc_q, delta = refs
        acc_kv[...] = jnp.zeros(acc_kv.shape, F32)
    acc_q[...] = jnp.zeros(acc_q.shape, F32)
    pick = lax.broadcasted_iota(jnp.int32, (8, width), 1) // HEAD_DIM
    pick = (pick == lax.broadcasted_iota(jnp.int32, (8, width), 0)).astype(F32)
    for part in range(count):
        at = slice(part * BLOCK, (part + 1) * BLOCK)
        product = gc[at, :].astype(F32) * ctx[at, :].astype(F32)
        delta[0, part] = lax.dot_general(
            pick, product, (((1,), (1,)), ((), ())), precision=lax.Precision.HIGHEST, preferred_element_type=F32
        )
        delta[1, part] = log[:, at]

    def step(pair, carry):
        k = pair // count
        q = pair % count

        @pl.when(flags[k * blocks + first + q] > 0)
        def _():
            key_rows = pl.ds(pl.multiple_of(k * BLOCK, BLOCK), BLOCK)
            query_rows = pl.ds(pl.multiple_of((first + q) * BLOCK, BLOCK), BLOCK)
            own_rows = pl.ds(pl.multiple_of(q * BLOCK, BLOCK), BLOCK)
            same = seg_col[key_rows, :] == seg_row[first + q]
            delta_rows = delta[0, q]
            log_rows = delta[1, q]
            for h in range(heads):
                at_q = slice(h * HEAD_DIM, (h + 1) * HEAD_DIM)
                at_k = slice(width + h * HEAD_DIM, width + (h + 1) * HEAD_DIM)
                at_v = slice(2 * width + h * HEAD_DIM, 2 * width + (h + 1) * HEAD_DIM)
                query = (qkv[query_rows, at_q] * 0.125).astype(BF)
                keys = qkv[key_rows, at_k]
                out = gc[own_rows, at_q]
                scores = block_dot(keys, query, ((1,), (1,)))
                weights = jnp.where(same, jnp.exp(jnp.where(same, scores, -1e30) - log_rows[h : h + 1, :]), 0.0)
                grad_weights = block_dot(qkv[key_rows, at_v], out, ((1,), (1,)))
                grad_scores = (weights * (grad_weights - delta_rows[h : h + 1, :])).astype(BF)
                acc_kv[key_rows, at_k] += block_dot(weights.astype(BF), out, ((1,), (0,)))
                acc_kv[key_rows, at_q] += block_dot(grad_scores, query, ((1,), (0,)))
                acc_q[own_rows, at_q] += block_dot(grad_scores, keys, ((0,), (0,)))

        return carry

    lax.fori_loop(0, blocks * count, step, 0)
    grad_q = (acc_q[...] * 0.125).astype(BF)
    if resumed:
        grad[:half, :width] = before_q[...]
        grad[half:, :width] = grad_q
        grad[:, width:] = acc_kv[...].astype(BF)
    else:
        out_q[...] = grad_q


def attention_backward(flags, qkv, seg_col, seg_row, log, context, grad, width, before=()):
    tokens = qkv.shape[0]
    half = tokens // 2
    resumed = len(before) > 0
    scratch = [pltpu.VMEM((half, width), F32), pltpu.VMEM((2, half // BLOCK, 8, BLOCK), F32)]
    if resumed:
        out_shape = jax.ShapeDtypeStruct((tokens, 3 * width), BF)
        scratch.insert(1, pltpu.VMEM((tokens, 2 * width), F32))
    else:
        out_shape = (jax.ShapeDtypeStruct((half, width), BF), jax.ShapeDtypeStruct((tokens, 2 * width), F32))
    return pl.pallas_call(
        partial(backward_kernel, first=half // BLOCK if resumed else 0, resumed=resumed, width=width),
        out_shape=out_shape,
        in_specs=[pl.BlockSpec(memory_space=pltpu.SMEM)] + [pl.BlockSpec(memory_space=pltpu.VMEM)] * (6 + len(before)),
        scratch_shapes=scratch,
        cost_estimate=pl.CostEstimate(flops=8 * 10**9, transcendentals=3 * 10**6, bytes_accessed=8 * 10**6),
        name="attention_backward_other" if resumed else "attention_backward_own",
    )(flags, qkv, seg_col, seg_row, log, context, grad, *before)


def shards(
    inputs,
    segment_ids,
    cotangent,
    w_query,
    w_key,
    w_value,
    b_query,
    b_value,
    w_out,
    b_out,
    gain_one,
    shift_one,
    w_up,
    b_up,
    w_down,
    b_down,
    gain_two,
    shift_two,
):
    ranks = lax.axis_size("tensor")
    rank = lax.axis_index("tensor")
    which = rank % 2
    rows = inputs.shape[1]
    half = 2 * rows
    width = w_query.shape[1]
    hidden_width = w_up.shape[1]
    model = inputs.shape[2]

    def inner(x):
        return lax.ppermute(x, "tensor", [(i, i ^ 1) for i in range(ranks)])

    def outer(x):
        return lax.ppermute(x, "tensor", [(i, i ^ 2) for i in range(ranks)])

    groups = lax.axis_size("dp")
    group = lax.axis_index("dp")

    def across(x, mask):
        return lax.ppermute(x, "dp", [(i, i ^ mask) for i in range(groups)])

    def sum_groups(x, order, gates):
        marks = []
        for shift, count in order:
            x = x + gates[0] if len(marks) == 1 else x
            own = (group >> shift) % count
            part = x.shape[0] // count
            total = lax.dynamic_slice_in_dim(x, own * part, part)
            for j in range(1, count):
                send = lax.dynamic_slice_in_dim(x, (own ^ j) * part, part).astype(BF)
                total = total + across(send, j << shift).astype(F32)
            x = total
            marks.append(x[0, 0])
        x = x.astype(BF)
        for shift, count in reversed(order):
            x = x + gates[-1].astype(BF) if shift == 0 else x
            own = (group >> shift) % count
            part = x.shape[0]
            whole = jnp.zeros((part * count,) + x.shape[1:], BF)
            whole = lax.dynamic_update_slice_in_dim(whole, x, own * part, 0)
            for j in range(1, count):
                whole = lax.dynamic_update_slice_in_dim(whole, across(x, j << shift), (own ^ j) * part, 0)
            x = whole
        return x, marks

    def to_sequence(x):
        kept = jnp.where(which == 0, x[0], x[1])
        got = inner(jnp.where(which == 0, x[1], x[0]))
        return jnp.where(which == 0, jnp.concatenate([kept, got]), jnp.concatenate([got, kept]))

    def from_sequence(x):
        low, high = x[:rows], x[rows:]
        kept = jnp.where(which == 0, low, high)
        got = inner(jnp.where(which == 0, high, low))
        return jnp.where(which == 0, jnp.stack([kept, got]), jnp.stack([got, kept]))

    own_in = to_sequence(inputs)
    straight = outer(jnp.where(which == 0, inputs[0], inputs[1]))
    crossed = jnp.where(which == 0, inputs[1], inputs[0])
    crossed = lax.ppermute(crossed, "tensor", [(i, i ^ 3) for i in range(ranks)])
    other_in = jnp.where(
        which == 0, jnp.concatenate([straight, crossed]), jnp.concatenate([crossed, straight])
    )
    own_cot = to_sequence(cotangent).astype(F32)

    def both(x, axis):
        return jnp.concatenate([x, inner(x)], axis)

    wqkv = both(jnp.concatenate([w_query, w_key, w_value], 1)[None], 0)
    wqkv = wqkv.reshape(2, model, 3, width).transpose(1, 2, 0, 3).reshape(model, 3 * 2 * width)
    bias = both(jnp.stack([b_query, b_value])[None], 0).transpose(1, 0, 2).reshape(2, 2 * width)
    bias_qkv = jnp.concatenate([bias[0], jnp.zeros((2 * width,), F32), bias[1]])
    w_out2 = both(w_out, 0)
    w_up2 = both(w_up, 1)
    b_up2 = both(b_up, 0)
    w_down2 = both(w_down, 0)

    segments = jnp.where(which == 0, segment_ids[0], segment_ids[1])
    first = jnp.where(rank // 2 == 0, segments[:half], segments[half:])
    second = jnp.where(rank // 2 == 0, segments[half:], segments[:half])
    seg = jnp.concatenate([first, second])

    blocked = seg.reshape(-1, BLOCK)
    low_id, high_id = blocked[:, 0], blocked[:, -1]
    flags = (low_id[:, None] <= high_id[None, :]) & (low_id[None, :] <= high_id[:, None])
    flags = flags.astype(jnp.int32).reshape(-1)
    seg_col = seg[:, None]
    seg_row = seg.reshape(-1, 1, BLOCK)

    def project(x):
        return (mm(x, wqkv) + bias_qkv).astype(BF)

    qkv_own = project(own_in)
    state = attention_forward(
        flags, qkv_own, seg_col, seg_row, 2 * width, "attention_own_own", 0, (0, 1), final=False
    )
    qkv = jnp.concatenate([qkv_own, project(other_in)])
    context_other, log_other = attention_forward(
        flags, qkv, seg_col, seg_row, 2 * width, "attention_other_all", 1, (0, 2), after=state[:1]
    )
    got = outer(mm(context_other, w_out2).astype(BF))
    context_own, log_own = attention_forward(
        flags, qkv, seg_col, seg_row, 2 * width, "attention_own_other", 0, (1, 2), state=state
    )
    attended = mm(context_own, w_out2) + got.astype(F32) + b_out
    normal_one, inverse_one = normalize(own_in.astype(F32) + attended)
    hidden_one = normal_one * gain_one + shift_one
    low_own = hidden_one.astype(BF)
    low_other = outer(low_own)

    def feed(low):
        value, slope = gelu_pair(mm(low, w_up2) + b_up2)
        return value.astype(BF), slope

    act_own, slope_own = feed(low_own)
    act_other, slope_other = feed(low_other)
    got = outer(mm(act_other, w_down2).astype(BF))
    branch = mm(act_own, w_down2) + got.astype(F32) + b_down
    normal_two, inverse_two = normalize(hidden_one + branch)
    output = (normal_two * gain_two + shift_two).astype(BF)

    grad_two, grad_gain_two, grad_shift_two = norm_backward(own_cot, gain_two, normal_two, inverse_two)
    gb_own = grad_two.astype(BF)
    grad_b_down = jnp.sum(gb_own.astype(F32), 0)
    gb_other = outer(gb_own)
    before_own = (mm_t(gb_own, w_down2) * slope_own).astype(BF)
    before_other = (mm_t(gb_other, w_down2) * slope_other).astype(BF)
    partial_up = mm_t(before_other, w_up2).astype(BF)
    got = outer(partial_up)
    grad_w_down = t_mm(act_own, gb_own) + t_mm(act_other, gb_other)
    grad_w_up = t_mm(low_own, before_own) + t_mm(low_other, before_other)
    grad_b_up = jnp.sum(before_own.astype(F32), 0) + jnp.sum(before_other.astype(F32), 0)

    def pair_sum(mine, theirs, gate=0.0):
        return mine + inner((theirs + gate).astype(BF)).astype(F32)

    def zero_after(x):
        return jnp.where(x != x, 1.0, 0.0).astype(F32)

    gate = zero_after(partial_up[0, 0])
    grad_w_up = pair_sum(grad_w_up[:, :hidden_width], grad_w_up[:, hidden_width:], gate).astype(BF)
    grad_w_down = pair_sum(grad_w_down[:hidden_width], grad_w_down[hidden_width:], gate).astype(BF)
    grad_w_up, grad_w_down = lax.psum((grad_w_up, grad_w_down), "dp")
    grad_hidden = mm_t(before_own, w_up2) + got.astype(F32) + grad_two
    grad_one, grad_gain_one, grad_shift_one = norm_backward(grad_hidden, gain_one, normal_one, inverse_one)
    ga_own = grad_one.astype(BF)
    grad_b_out = jnp.sum(ga_own.astype(F32), 0)
    ga_other = outer(ga_own)

    grad_w_out = t_mm(context_own, ga_own) + t_mm(context_other, ga_other)
    order = [(0, 2)] + [(i, min(4, groups >> i)) for i in range(1, groups.bit_length() - 1, 2)]

    gc_own = mm_t(ga_own, w_out2).astype(BF)
    gc_other = mm_t(ga_other, w_out2).astype(BF)
    before = attention_backward(flags, qkv, seg_col, seg_row, log_own, context_own, gc_own, 2 * width)
    gqkv = attention_backward(
        flags, qkv, seg_col, seg_row, log_other, context_other, gc_other, 2 * width, before=before
    )
    gqkv_own, gqkv_other = gqkv[:half], gqkv[half:]
    partial_other = mm_t(gqkv_other, wqkv).astype(BF)
    got = outer(partial_other)
    grad_wqkv = t_mm(gqkv_own, own_in) + t_mm(gqkv_other, other_in)
    grad_bqkv = jnp.sum(gqkv_own.astype(F32), 0) + jnp.sum(gqkv_other.astype(F32), 0)

    shared = jnp.stack(
        [grad_b_out, grad_gain_one, grad_shift_one, grad_b_down, grad_gain_two, grad_shift_two]
    )
    shared = shared + inner(shared)
    shared = shared + outer(shared)

    by_part = grad_wqkv.reshape(3, 2, width, model)
    bias_parts = grad_bqkv.reshape(3, 2, width)
    up_rows = hidden_width // model
    parts = []
    for i in range(2):
        line = jnp.concatenate([bias_parts[0, i], bias_parts[2, i], jnp.zeros((model - 2 * width,), F32)])
        up_part = grad_b_up[i * hidden_width : (i + 1) * hidden_width].reshape(up_rows, model)
        weights = [by_part[0, i], by_part[1, i], by_part[2, i], grad_w_out[i * width : (i + 1) * width]]
        parts.append(jnp.concatenate(weights + [up_part, line[None]]))
    used = parts[0].shape[0] + 6
    unit = max(128, 2 * groups)
    rest = jnp.zeros((-used % unit, model), F32)
    payload = jnp.concatenate([pair_sum(*parts), shared, rest])
    summed, started = sum_groups(
        payload,
        order,
        (
            zero_after(partial_other[0, 0]),
            zero_after(grad_w_up[0, 0]) + zero_after(grad_w_down[0, 0]),
        ),
    )
    grad_input = mm_t(gqkv_own, wqkv) + got.astype(F32) + (grad_one + zero_after(started[1]))
    grad_qkv = summed[: 4 * width].astype(F32)
    bias_rows = summed[4 * width : used].astype(F32)
    small = jnp.concatenate([bias_rows[up_rows, : 2 * width], bias_rows[:up_rows].reshape(-1)])
    shared = bias_rows[up_rows + 1 :]

    return (
        from_sequence(output),
        from_sequence(grad_input),
        grad_qkv[:width].T,
        grad_qkv[width : 2 * width].T,
        grad_qkv[2 * width : 3 * width].T,
        small[:width],
        small[width : 2 * width],
        grad_qkv[3 * width :],
        shared[0],
        shared[1],
        shared[2],
        grad_w_up.astype(F32),
        small[2 * width :],
        grad_w_down.astype(F32),
        shared[3],
        shared[4],
        shared[5],
    )


def solution(mesh):
    tokens = P("dp", "tensor", None)
    columns = P(None, "tensor")
    lines = P("tensor", None)
    split = P("tensor")
    whole = P()
    return jax.shard_map(
        shards,
        mesh=mesh,
        in_specs=(tokens, P("dp", None), tokens, columns, columns, columns, split, split, lines)
        + (whole, whole, whole, columns, split, lines, whole, whole, whole),
        out_specs=(tokens, tokens, columns, columns, columns, split, split, lines, whole, whole, whole)
        + (columns, split, lines, whole, whole, whole),
        check_vma=False,
    )
```
